128 devices in a mesh: section: 4 (over y), dp: 32 (over x, z, core).
Axes of the slice: x: 4, y: 4, z: 4, core: 2. Of those that a mesh axis runs over, the one named last changes fastest.
Arguments:
- tokens: bfloat16 [8192, 4096], P('dp'), may hold values from -6 to 6
- cotangent: bfloat16 [8192, 4096], P('dp'), may hold values from -30 to 30
- lengths: int32 [128], P('dp'), may hold values from 1 to 64
- seq_user: int32 [128], P('dp'), may hold values from 0 to 63, as said below
- norm_gains: float32 [4, 4096], P('section'), may hold values from 0.5 to 1.5
- weights: float32 [4, 4096, 2, 256], P('section', 'dp'), may hold values from -1 to 1
- first_moment: float32 [4, 4096, 2, 256], P('section', 'dp'), may hold values from -6 to 6
- second_moment: float32 [4, 4096, 2, 256], P('section', 'dp'), may hold values from 0.25 to 4
Outputs:
- new_first: float32 [4, 4096, 2, 256], P('section', 'dp')
- new_second: float32 [4, 4096, 2, 256], P('section', 'dp')
- step_dir: float32 [4, 4096, 2, 256], P('section', 'dp')
- user_ratio: float32 [64], P('dp')
The draws below stay inside these ranges and needn't reach their ends.
Inputs may be any that keep to these rules, and one draw needn't show every extreme that they name: `seq_user`: the i-th block of 4 sequences carries only the user ids i * 2 to i * 2 + 1, each of them at least once.
All inputs are finite; a program needn't handle non-finite values.
Results may differ from the reference program's by a relative error of at most 0.0045.
Values may be sent and summed in bfloat16 or wider, within the bound.
No kernel may reach another device: no remote copies, remote signals or barrier semaphores. Data moves between devices by JAX's collectives and lax.ppermute only.
A program may use at most 128 MiB of HBM per device.

```python
import math
import jax
import jax.numpy as jnp
from jax import lax

D = 4096
K = 256
SEQLEN = 64
SEQS_DEV = 4
TOK_DEV = 256
USERS_DEV = 2
SEQS = 128
TOKENS = 8192
USERS = 64
SECTIONS = 4
N_SECTION = 4
N_DP = 32


def draw_cotangent(key, part):
    key_one, key_two, key_three = jax.random.split(key, 3)
    base_values = jnp.clip(jax.random.normal(key_one, (TOKENS, D), jnp.float32), -5.0, 5.0)
    row_scale = jnp.exp(jax.random.uniform(key_two, (TOKENS, 1), jnp.float32, math.log(0.3), math.log(3.0)))
    col_scale = jnp.exp(jax.random.uniform(key_three, (1, D), jnp.float32, math.log(0.5), math.log(2.0)))
    return (base_values * row_scale * col_scale).astype(jnp.bfloat16)


def draw_lengths(key, part):
    drawn_lengths = jax.random.randint(key, (SEQS,), 1, SEQLEN + 1)
    return drawn_lengths.at[0].set(SEQLEN).astype(jnp.int32)


def draw_seq_user(key, part):
    devices = SEQS // SEQS_DEV
    device_keys = jax.random.split(key, devices)

    def one_device(device_key, device_no):
        key_one, key_two = jax.random.split(device_key)
        extra_users = jax.random.randint(key_one, (SEQS_DEV,), 0, USERS_DEV)
        slots = jnp.arange(SEQS_DEV)
        base_users = jnp.where(slots < USERS_DEV, slots, extra_users)
        shuffled = jax.random.permutation(key_two, base_users)
        return (shuffled + device_no * USERS_DEV).astype(jnp.int32)
    return jax.vmap(one_device)(device_keys, jnp.arange(devices)).reshape(SEQS).astype(jnp.int32)


def draw_weights(key, part):
    normal_raw = jnp.clip(jax.random.normal(key, (SECTIONS, D, 2, K), jnp.float32), -6.0, 6.0)
    column_scale = jnp.array([D ** (-0.5), K ** (-0.5)], jnp.float32)
    return normal_raw * column_scale[None, None, :, None]


def block_scale(rng, shape, cuts, low, high):
    def one(axis_at, shards_of):
        heights = jax.random.uniform(jax.random.fold_in(jax.random.fold_in(rng, 6), axis_at), (shards_of,), jnp.float32, low / len(cuts), high / len(cuts))
        return jnp.repeat(jnp.exp(heights), shape[axis_at] // shards_of).reshape((-1,) + (1,) * (len(shape) - axis_at - 1))

    loudness = one(*cuts[0])
    for cut in cuts[1:]:
        loudness = loudness * one(*cut)
    return loudness


def centred(rng, dims, scale, bound, cuts=(), dtype=jnp.bfloat16):
    result = jax.random.normal(rng, dims, jnp.float32) * scale
    if len(cuts) > 0:
        result = block_scale(rng, dims, cuts, -0.22, 0.18) * result
    return jnp.clip(result, min=-bound, max=bound).astype(dtype)


def setup_inputs(seed: int = 0) -> dict:
    streams_of = jax.random.split(jax.random.key(seed), 9)
    return {
        "tokens": centred(streams_of[0], (TOKENS, D), 1.0, 6.0, ((0, 32),)),
        "cotangent": draw_cotangent(jax.random.fold_in(streams_of[8], 71), 0),
        "lengths": draw_lengths(jax.random.fold_in(streams_of[8], 71), 0),
        "seq_user": draw_seq_user(jax.random.fold_in(streams_of[8], 71), 0),
        "norm_gains": jnp.clip(1.0 + 0.1 * jax.random.normal(streams_of[4], (SECTIONS, D), jnp.float32), 0.5, 1.5),
        "weights": draw_weights(jax.random.fold_in(streams_of[8], 71), 0),
        "first_moment": centred(streams_of[6], (SECTIONS, D, 2, K), 1.0, 6.0, ((0, 4), (1, 32)), jnp.float32),
        "second_moment": jnp.clip(jnp.exp(math.log(4.0) - 2.7725887 * jax.random.uniform(streams_of[7], (SECTIONS, D, 2, K), jnp.float32) ** block_scale(streams_of[7], (SECTIONS, D, 2, K), ((0, 4), (1, 32)), -0.2, 0.2)), 0.25, 4.0),
    }


CLIP_BOUND = 70000.0
LOSS_SCALE = 1024.0
BETA_ONE = 0.9
BETA_TWO = 0.999
FIRST_FIX = 1.0 - 0.9 ** 50
SECOND_FIX = 1.0 - 0.999 ** 50
ADAM_EPS = 1e-08
NORM_EPS = 1e-05

def section_forward(hidden, section_gain, down_cast, up_cast):
    widened = hidden.astype(jnp.float32)
    inverse = lax.rsqrt(lax.optimization_barrier(jnp.mean(widened * widened, axis=-1, keepdims=True)) + NORM_EPS)
    normed = (widened * inverse * section_gain).astype(jnp.bfloat16)
    inner_act = jnp.dot(normed, down_cast, preferred_element_type=jnp.float32)
    active = jax.nn.silu(inner_act).astype(jnp.bfloat16)
    branch = lax.dot_general(active, up_cast, (((1,), (1,)), ((), ())), preferred_element_type=jnp.float32)
    return ((widened + branch).astype(jnp.bfloat16), (widened, inverse, normed, inner_act, active))

def section_backward(grad_out, section_gain, down_cast, up_cast, kept_acts):
    widened, inverse, normed, inner_act, active = kept_acts
    grad_active = jnp.dot(grad_out, up_cast, preferred_element_type=jnp.float32)
    sigmoid_val = jax.nn.sigmoid(inner_act)
    grad_inner = (grad_active * sigmoid_val * (1.0 + inner_act * (1.0 - sigmoid_val))).astype(jnp.bfloat16)
    grad_normed = lax.dot_general(grad_inner, down_cast, (((1,), (1,)), ((), ())), preferred_element_type=jnp.float32)
    scaled = grad_normed * section_gain
    projected = lax.optimization_barrier(jnp.mean(scaled * widened, axis=-1, keepdims=True))
    grad_in = grad_out.astype(jnp.float32) + inverse * scaled - widened * inverse * inverse * inverse * projected
    return (grad_in.astype(jnp.bfloat16), grad_inner)

def gram_of(values):
    return lax.dot_general(values, values, (((1,), (1,)), ((), ())), preferred_element_type=jnp.float32)

def user_squares(normed, grad_inner, active, grad_out, owners):
    joint = gram_of(normed) * gram_of(grad_inner) + gram_of(active) * gram_of(grad_out)
    spread = jnp.dot(joint, owners, precision=lax.Precision.HIGHEST)
    return lax.optimization_barrier(jnp.sum(spread * owners, axis=0))

def reference(tokens, cotangent, lengths, seq_user, norm_gains, weights, first_moment, second_moment):
    low_weights = weights.astype(jnp.bfloat16)
    hidden = tokens
    saved_all = []
    for section_no in range(N_SECTION):
        hidden, kept_acts = section_forward(hidden, norm_gains[section_no], low_weights[section_no, :, 0, :], low_weights[section_no, :, 1, :])
        saved_all.append(kept_acts)
    positions = jnp.arange(TOKENS) % SEQLEN
    usable = positions < jnp.repeat(lengths, SEQLEN)
    token_user = jnp.repeat(seq_user, SEQLEN)
    owners = ((token_user[:, None] == jnp.arange(USERS)[None, :]) & usable[:, None]).astype(jnp.float32)
    grad_out = cotangent * usable[:, None].astype(jnp.bfloat16)
    records = [None] * N_SECTION
    for section_no in reversed(range(N_SECTION)):
        grad_in, grad_inner = section_backward(grad_out, norm_gains[section_no], low_weights[section_no, :, 0, :], low_weights[section_no, :, 1, :], saved_all[section_no])
        records[section_no] = (grad_out, grad_inner)
        grad_out = grad_in
    squares = jnp.zeros((USERS,), jnp.float32)
    owner_blocks = owners.reshape(N_DP, TOK_DEV, USERS)
    for section_no in range(N_SECTION):
        members = (saved_all[section_no][2].reshape(N_DP, TOK_DEV, D), records[section_no][1].reshape(N_DP, TOK_DEV, K), saved_all[section_no][4].reshape(N_DP, TOK_DEV, K), records[section_no][0].reshape(N_DP, TOK_DEV, D), owner_blocks)
        per_device = lax.map(lambda group_in: user_squares(*group_in), members)
        squares = squares + lax.optimization_barrier(jnp.sum(per_device, axis=0))
    user_norm = jnp.sqrt(squares)
    user_ratio = user_norm / CLIP_BOUND
    factors = LOSS_SCALE / jnp.maximum(user_norm, CLIP_BOUND)
    token_factor = jnp.dot(owners, factors, precision=lax.Precision.HIGHEST)
    grads_all = []
    for section_no in range(N_SECTION):
        grad_out, grad_inner = records[section_no]
        weighted_inner = (grad_inner.astype(jnp.float32) * token_factor[:, None]).astype(jnp.bfloat16)
        weighted_out = (grad_out.astype(jnp.float32) * token_factor[:, None]).astype(jnp.bfloat16)
        down_term = lax.dot_general(saved_all[section_no][2], weighted_inner, (((0,), (0,)), ((), ())), preferred_element_type=jnp.float32)
        up_term = lax.dot_general(weighted_out, saved_all[section_no][4], (((0,), (0,)), ((), ())), preferred_element_type=jnp.float32)
        grads_all.append(jnp.stack([down_term, up_term], axis=1))
    gradient = jnp.stack(grads_all, axis=0)
    new_first = BETA_ONE * first_moment + (1.0 - BETA_ONE) * gradient
    new_second = BETA_TWO * second_moment + (1.0 - BETA_TWO) * gradient * gradient
    step_dir = new_first / FIRST_FIX / (jnp.sqrt(new_second / SECOND_FIX) + ADAM_EPS)
    return (new_first, new_second, step_dir, user_ratio)
```

```python
import jax
import jax.numpy as jnp
from jax import lax
from jax.sharding import PartitionSpec as P

SEQLEN = 64
USERS_DEV = 2
SECTIONS = 4


CLIP_BOUND = 70000.0
LOSS_SCALE = 1024.0
BETA_ONE = 0.9
BETA_TWO = 0.999
FIRST_FIX = 1.0 - 0.9**50
SECOND_FIX = 1.0 - 0.999**50
ADAM_EPS = 1e-08
NORM_EPS = 1e-05


def section_forward(hidden, section_gain, down_cast, up_cast, last):
    widened = hidden.astype(jnp.float32)
    inverse = lax.rsqrt(jnp.mean(widened * widened, axis=-1, keepdims=True) + NORM_EPS)
    normed = (widened * inverse * section_gain).astype(jnp.bfloat16)
    inner_act = jnp.dot(normed, down_cast, preferred_element_type=jnp.float32)
    active = jax.nn.silu(inner_act).astype(jnp.bfloat16)
    kept = (hidden, inverse, normed, inner_act, active)
    if last:
        return None, kept
    branch = lax.dot_general(
        active, up_cast, (((1,), (1,)), ((), ())), preferred_element_type=jnp.float32
    )
    return (widened + branch).astype(jnp.bfloat16), kept


def section_backward(grad_out, section_gain, down_cast, up_cast, kept, first):
    hidden, inverse, normed, inner_act, active = kept
    grad_active = jnp.dot(grad_out, up_cast, preferred_element_type=jnp.float32)
    sigmoid_val = jax.nn.sigmoid(inner_act)
    grad_inner = (grad_active * sigmoid_val * (1.0 + inner_act * (1.0 - sigmoid_val))).astype(
        jnp.bfloat16
    )
    if first:
        return None, grad_inner
    widened = hidden.astype(jnp.float32)
    grad_normed = lax.dot_general(
        grad_inner, down_cast, (((1,), (1,)), ((), ())), preferred_element_type=jnp.float32
    )
    scaled = grad_normed * section_gain
    projected = jnp.mean(scaled * widened, axis=-1, keepdims=True)
    grad_in = (
        grad_out.astype(jnp.float32)
        + inverse * scaled
        - widened * inverse * inverse * inverse * projected
    )
    return grad_in.astype(jnp.bfloat16), grad_inner


def gram_of(values):
    return lax.dot_general(
        values, values, (((1,), (1,)), ((), ())), preferred_element_type=jnp.float32
    )


def on_device(
    tokens, cotangent, lengths, seq_user, norm_gains, weights, first_moment, second_moment
):
    section_index = lax.axis_index("section")
    dp_index = lax.axis_index("dp")
    dp_count = lax.axis_size("dp")
    chips = dp_count // 2
    core = dp_index % 2
    tok_rows = tokens.shape[0]
    rows = weights.shape[1]
    width = weights.shape[3]

    gains = lax.all_gather(norm_gains, "section", axis=0, tiled=True)
    shard = weights[0].astype(jnp.bfloat16).transpose(1, 0, 2)
    column = lax.all_gather(shard, "section", axis=0, tiled=True)
    packed = lax.all_gather(column, "dp", axis=1, tiled=True)

    positions = jnp.arange(tok_rows) % SEQLEN
    usable = positions < jnp.repeat(lengths, SEQLEN)
    local_user = seq_user - dp_index * USERS_DEV
    token_user = jnp.repeat(local_user, SEQLEN)
    owners = ((token_user[:, None] == jnp.arange(USERS_DEV)[None, :]) & usable[:, None]).astype(
        jnp.float32
    )
    hidden = tokens
    saved = []
    for section in range(SECTIONS):
        hidden, kept = section_forward(
            hidden,
            gains[section],
            packed[2 * section],
            packed[2 * section + 1],
            section == SECTIONS - 1,
        )
        saved.append(kept)
    grad_out = cotangent * usable[:, None].astype(jnp.bfloat16)
    records = [None] * SECTIONS
    for section in reversed(range(SECTIONS)):
        grad_in, grad_inner = section_backward(
            grad_out,
            gains[section],
            packed[2 * section],
            packed[2 * section + 1],
            saved[section],
            section == 0,
        )
        records[section] = (grad_out, grad_inner)
        grad_out = grad_in
    joint = jnp.zeros((tok_rows, tok_rows), jnp.float32)
    for section in range(SECTIONS):
        joint += gram_of(saved[section][2]) * gram_of(records[section][1])
        joint += gram_of(saved[section][4]) * gram_of(records[section][0])
    spread = jnp.dot(joint, owners, precision=lax.Precision.HIGHEST)
    squares = jnp.sum(spread * owners, axis=0)
    user_norm = jnp.sqrt(squares)
    factors = LOSS_SCALE / jnp.maximum(user_norm, CLIP_BOUND)
    token_factor = jnp.dot(owners, factors, precision=lax.Precision.HIGHEST)[:, None]

    def mine(arrays):
        return lax.dynamic_index_in_dim(jnp.stack(arrays), section_index, 0, keepdims=False)

    normed = mine([saved[s][2] for s in range(SECTIONS)])
    active = mine([saved[s][4] for s in range(SECTIONS)])
    grad_out = mine([records[s][0] for s in range(SECTIONS)])
    grad_inner = mine([records[s][1] for s in range(SECTIONS)])
    weighted_inner = (grad_inner.astype(jnp.float32) * token_factor).astype(jnp.bfloat16)
    weighted_out = (grad_out.astype(jnp.float32) * token_factor).astype(jnp.bfloat16)
    down_term = lax.dot_general(
        normed, weighted_inner, (((0,), (0,)), ((), ())), preferred_element_type=jnp.float32
    )
    up_term = lax.dot_general(
        weighted_out, active, (((0,), (0,)), ((), ())), preferred_element_type=jnp.float32
    )
    both = jnp.concatenate([down_term, up_term], axis=1).reshape(chips, 2, rows, 2 * width)
    keep = lax.dynamic_index_in_dim(both, core, 1, keepdims=False)
    give = lax.dynamic_index_in_dim(both, 1 - core, 1, keepdims=False).astype(jnp.bfloat16)
    partner = lax.ppermute(give, "dp", [(d, d ^ 1) for d in range(dp_count)])
    paired = (keep + partner.astype(jnp.float32)).astype(jnp.bfloat16)
    groups = [[2 * chip + c for chip in range(chips)] for c in range(2)]
    pieces = lax.all_to_all(paired, "dp", 0, 0, axis_index_groups=groups)
    gradient = jnp.sum(pieces.astype(jnp.float32), axis=0).reshape(rows, 2, width)
    moment_one = BETA_ONE * first_moment[0] + (1.0 - BETA_ONE) * gradient
    moment_two = BETA_TWO * second_moment[0] + (1.0 - BETA_TWO) * gradient * gradient
    direction = moment_one / FIRST_FIX / (jnp.sqrt(moment_two / SECOND_FIX) + ADAM_EPS)
    return (moment_one[None], moment_two[None], direction[None], user_norm / CLIP_BOUND)


def solution(mesh):
    return jax.shard_map(
        on_device,
        mesh=mesh,
        in_specs=(
            P("dp", None),
            P("dp", None),
            P("dp"),
            P("dp"),
            P("section", None),
            P("section", "dp", None, None),
            P("section", "dp", None, None),
            P("section", "dp", None, None),
        ),
        out_specs=(
            P("section", "dp", None, None),
            P("section", "dp", None, None),
            P("section", "dp", None, None),
            P("dp"),
        ),
        check_vma=False,
    )
```

```python
import functools

import jax
import jax.numpy as jnp
from jax import lax
from jax.experimental import pallas as pl
from jax.experimental.pallas import tpu as pltpu
from jax.sharding import PartitionSpec as P

SEQLEN = 64
USERS_DEV = 2
SECTIONS = 4
CHUNK = 1024

CLIP_BOUND = 70000.0
LOSS_SCALE = 1024.0
BETA_ONE = 0.9
BETA_TWO = 0.999
FIRST_FIX = 1.0 - 0.9**50
SECOND_FIX = 1.0 - 0.999**50
ADAM_EPS = 1e-08
NORM_EPS = 1e-05

F32 = jnp.float32
BF16 = jnp.bfloat16


def dot_nn(a, b):
    return jnp.dot(a, b, preferred_element_type=F32)


def dot_nt(a, b):
    return lax.dot_general(a, b, (((1,), (1,)), ((), ())), preferred_element_type=F32)


def chain_kernel(
    scal,
    tokens,
    normed0,
    gout3,
    gram_n0,
    gram_g3,
    inv0,
    gains,
    own_col,
    own_row,
    weights,
    keep,
    give,
    ratio,
    wv,
    hs,
    nm,
    go,
    inner,
    act,
    gin,
    acc,
    acc2,
    joint,
    sq,
    sems,
):
    rows, width = tokens.shape
    chunks = width // CHUNK

    def load(section, which):
        slot = scal[section]
        return pltpu.make_async_copy(
            weights.at[2 * slot + which],
            wv.at[2 * section + which],
            sems.at[2 * section + which],
        )

    for section in range(SECTIONS):
        for which in range(2):
            load(section, which).start()

    def cols(i):
        return pl.ds(pl.multiple_of(i * CHUNK, CHUNK), CHUNK)

    def each(body):
        def step(i, carry):
            body(cols(i))
            return carry

        lax.fori_loop(0, chunks, step, 0)

    inv = inv0[...]
    invs = [inv]
    for s in range(SECTIONS):
        load(s, 0).wait()
        slot = scal[s]
        if s == 0:
            value = dot_nn(normed0[...], wv[0])
        else:
            acc[...] = jnp.zeros_like(acc)
            acc2[...] = jnp.zeros_like(acc2)

            def norm_step(c, s=s, inv=inv, slot=slot):
                n = (hs[s - 1, :, c].astype(F32) * inv * gains[slot, :, c]).astype(BF16)
                nm[s - 1, :, c] = n
                acc[...] += dot_nn(n, wv[2 * s, c, :])
                acc2[...] += dot_nt(n, n)

            each(norm_step)
            value = acc[...]
            joint[s] = acc2[...]
        inner[s] = value
        active = (value * jax.nn.sigmoid(value)).astype(BF16)
        act[s] = active
        load(s, 1).wait()
        if s < SECTIONS - 1:
            sq[...] = jnp.zeros_like(sq)

            def up_step(c, s=s, active=active):
                old = tokens[:, c] if s == 0 else hs[s - 1, :, c]
                new = (old.astype(F32) + dot_nt(active, wv[2 * s + 1, c, :])).astype(BF16)
                hs[s, :, c] = new
                wide = new.astype(F32)
                wide = wide * wide
                part = wide[:, :128]
                for k in range(1, CHUNK // 128):
                    part = part + wide[:, 128 * k : 128 * (k + 1)]
                sq[...] += part

            each(up_step)
            mean = jnp.sum(sq[...], axis=-1, keepdims=True) * (1.0 / width)
            inv = lax.rsqrt(mean + NORM_EPS)
            invs.append(inv)

    total = jnp.zeros((rows, rows), F32)
    for s in reversed(range(SECTIONS)):
        if s == SECTIONS - 1:
            gact = dot_nn(gout3[...], wv[2 * s + 1])
            gram_g = gram_g3[...]
        else:
            gact = acc[...]
            gram_g = acc2[...]
        value = inner[s]
        sig = jax.nn.sigmoid(value)
        gi = (gact * sig * (1.0 + value * (1.0 - sig))).astype(BF16)
        gin[s] = gi
        gram_n = gram_n0[...] if s == 0 else joint[s]
        total = total + gram_n * dot_nt(gi, gi) + dot_nt(act[s], act[s]) * gram_g
        if s > 0:
            inv = invs[s]
            proj = jnp.sum(gi.astype(F32) * value, axis=-1, keepdims=True) * (1.0 / width)
            coef = inv * inv * proj
            slot = scal[s]
            acc[...] = jnp.zeros_like(acc)
            acc2[...] = jnp.zeros_like(acc2)

            def back_step(c, s=s, inv=inv, coef=coef, gi=gi, slot=slot):
                gn = dot_nt(gi, wv[2 * s, c, :])
                above = gout3[:, c] if s == SECTIONS - 1 else go[s, :, c]
                g = (
                    above.astype(F32)
                    + inv * (gn * gains[slot, :, c])
                    - hs[s - 1, :, c].astype(F32) * coef
                ).astype(BF16)
                go[s - 1, :, c] = g
                acc[...] += dot_nn(g, wv[2 * s - 1, c, :])
                acc2[...] += dot_nt(g, g)

            each(back_step)

    factor = jnp.zeros((rows, 1), F32)
    lane = lax.broadcasted_iota(jnp.int32, (1, 128), 1)
    report = jnp.zeros((1, 128), F32)
    for u in range(USERS_DEV):
        column = own_col[:, u : u + 1]
        part = jnp.sum(total * own_row[u : u + 1, :], axis=1, keepdims=True) * column
        norm = jnp.sqrt(jnp.sum(part, axis=0, keepdims=True))
        factor = factor + column * (LOSS_SCALE / jnp.maximum(norm, CLIP_BOUND))
        report = jnp.where(lane == u, norm * (1.0 / CLIP_BOUND), report)
    ratio[...] = jnp.broadcast_to(report, ratio.shape)

    me = scal[4]
    core = scal[5]
    wi = jnp.transpose(gin[me].astype(F32) * factor).astype(BF16)
    wa = jnp.transpose(act[me].astype(F32) * factor).astype(BF16)

    def emit(normed_of, gout_of):
        def step(q, carry):
            c = pl.ds(pl.multiple_of(q * 256, 256), 256)
            for half, (left, right) in enumerate(((wi, normed_of(c)), (wa, gout_of(c)))):
                both = dot_nn(left, right)
                low, high = both[:, :128], both[:, 128:]
                span = pl.ds(half * left.shape[0], left.shape[0])
                keep[q, span, :] = jnp.where(core == 0, low, high)
                give[q, span, :] = jnp.where(core == 0, high, low).astype(BF16)
            return carry

        lax.fori_loop(0, width // 256, step, 0)

    @pl.when(me == 0)
    def _():
        emit(lambda c: normed0[:, c], lambda c: go[0, :, c])

    @pl.when((me > 0) & (me < SECTIONS - 1))
    def _():
        emit(lambda c: nm[me - 1, :, c], lambda c: go[me, :, c])

    @pl.when(me == SECTIONS - 1)
    def _():
        emit(lambda c: nm[SECTIONS - 2, :, c], lambda c: gout3[:, c])


def run_chain(
    scal, tokens, normed0, gout3, gram_n0, gram_g3, inv0, gains, own_col, own_row, weights
):
    rows, width = tokens.shape
    inner_width = weights.shape[-1]
    blocks = width // 256
    vmem = pl.BlockSpec(memory_space=pltpu.VMEM)
    return pl.pallas_call(
        chain_kernel,
        out_shape=(
            jax.ShapeDtypeStruct((blocks, 2 * inner_width, 128), F32),
            jax.ShapeDtypeStruct((blocks, 2 * inner_width, 128), BF16),
            jax.ShapeDtypeStruct((8, 128), F32),
        ),
        in_specs=[pl.BlockSpec(memory_space=pltpu.SMEM)]
        + [vmem] * 9
        + [pl.BlockSpec(memory_space=pl.ANY)],
        out_specs=(vmem, vmem, vmem),
        scratch_shapes=[
            pltpu.VMEM((2 * SECTIONS, width, inner_width), BF16),
            pltpu.VMEM((SECTIONS - 1, rows, width), BF16),
            pltpu.VMEM((SECTIONS - 1, rows, width), BF16),
            pltpu.VMEM((SECTIONS - 1, rows, width), BF16),
            pltpu.VMEM((SECTIONS, rows, inner_width), F32),
            pltpu.VMEM((SECTIONS, rows, inner_width), BF16),
            pltpu.VMEM((SECTIONS, rows, inner_width), BF16),
            pltpu.VMEM((rows, inner_width), F32),
            pltpu.VMEM((rows, rows), F32),
            pltpu.VMEM((SECTIONS, rows, rows), F32),
            pltpu.VMEM((rows, 128), F32),
            pltpu.SemaphoreType.DMA((2 * SECTIONS,)),
        ],
        compiler_params=pltpu.CompilerParams(vmem_limit_bytes=60 * 1024 * 1024),
        name="chain",
    )(scal, tokens, normed0, gout3, gram_n0, gram_g3, inv0, gains, own_col, own_row, weights)


def on_device(
    tokens, cotangent, lengths, seq_user, norm_gains, weights, first_moment, second_moment
):
    section_index = lax.axis_index("section")
    dp_index = lax.axis_index("dp")
    dp_count = lax.axis_size("dp")
    chips = dp_count // 2
    core = dp_index % 2
    tok_rows, model_width = tokens.shape
    rows = weights.shape[1]
    width = weights.shape[3]

    shard = weights[0].astype(BF16).transpose(1, 0, 2).reshape(2 * rows, width)
    gain = norm_gains[0]
    high = lax.reduce_precision(gain, 8, 7)
    middle = lax.reduce_precision(gain - high, 8, 7)
    low = gain - high - middle
    digits = jnp.stack([high, middle, low]).astype(BF16).reshape(-1, width)
    payload = jnp.concatenate([shard, digits], axis=0)
    held = [payload]
    for shift in range(1, SECTIONS):
        pairs = [(s, (s + shift) % SECTIONS) for s in range(SECTIONS)]
        held.append(lax.ppermute(payload, "section", pairs))
    column = jnp.stack([piece[: 2 * rows].reshape(2, rows, width) for piece in held])
    column = column.reshape(2 * SECTIONS, rows, width)
    packed = lax.all_gather(column, "dp", axis=1, tiled=True)
    gains = jnp.stack(
        [
            jnp.sum(piece[2 * rows :].astype(F32).reshape(3, model_width), axis=0, keepdims=True)
            for piece in held
        ]
    )
    slots = (section_index - jnp.arange(SECTIONS)) % SECTIONS
    scal = jnp.concatenate([slots, section_index[None], core[None]]).astype(jnp.int32)

    positions = jnp.arange(tok_rows) % SEQLEN
    usable = positions < jnp.repeat(lengths, SEQLEN)
    token_user = jnp.repeat(seq_user - dp_index * USERS_DEV, SEQLEN)
    own_row = (
        (token_user[None, :] == jnp.arange(8)[:, None])
        & usable[None, :]
        & (jnp.arange(8) < USERS_DEV)[:, None]
    ).astype(F32)
    own_col = (
        (token_user[:, None] == jnp.arange(128)[None, :])
        & usable[:, None]
        & (jnp.arange(128) < USERS_DEV)[None, :]
    ).astype(F32)
    widened = tokens.astype(F32)
    inv0 = lax.rsqrt(jnp.mean(widened * widened, axis=-1, keepdims=True) + NORM_EPS)
    gain0 = lax.dynamic_index_in_dim(gains, slots[0], 0, keepdims=False)
    normed0 = (widened * inv0 * gain0).astype(BF16)
    gout3 = cotangent * usable[:, None].astype(BF16)
    keep, give, ratio = run_chain(
        scal,
        tokens,
        normed0,
        gout3,
        dot_nt(normed0, normed0),
        dot_nt(gout3, gout3),
        inv0,
        gains,
        own_col,
        own_row,
        packed,
    )
    partner = lax.ppermute(give, "dp", [(d, d ^ 1) for d in range(dp_count)])
    paired = (keep + partner.astype(F32)).astype(BF16)
    groups = [[2 * chip + c for chip in range(chips)] for c in range(2)]
    pieces = lax.all_to_all(paired, "dp", 0, 0, axis_index_groups=groups)
    gradient = jnp.sum(pieces.astype(F32), axis=0).reshape(2, width, rows).transpose(2, 0, 1)
    moment_one = BETA_ONE * first_moment[0] + (1.0 - BETA_ONE) * gradient
    moment_two = BETA_TWO * second_moment[0] + (1.0 - BETA_TWO) * gradient * gradient
    direction = moment_one / FIRST_FIX / (jnp.sqrt(moment_two / SECOND_FIX) + ADAM_EPS)
    return (moment_one[None], moment_two[None], direction[None], ratio[0, :USERS_DEV])


def solution(mesh):
    return jax.shard_map(
        on_device,
        mesh=mesh,
        in_specs=(
            P("dp", None),
            P("dp", None),
            P("dp"),
            P("dp"),
            P("section", None),
            P("section", "dp", None, None),
            P("section", "dp", None, None),
            P("section", "dp", None, None),
        ),
        out_specs=(
            P("section", "dp", None, None),
            P("section", "dp", None, None),
            P("section", "dp", None, None),
            P("dp"),
        ),
        check_vma=False,
    )
```

```python
import functools

import jax
import jax.numpy as jnp
from jax import lax
from jax.experimental import pallas as pl
from jax.experimental.pallas import tpu as pltpu
from jax.sharding import PartitionSpec as P

SEQLEN = 64
USERS_DEV = 2
SECTIONS = 4
CHUNK = 1024
RING = 4
LAYOUT = ((0, 0, 4), (1, 0, 4), (3, 0, 4), (2, 0, 2), (2, 2, 4))
PIECES = len(LAYOUT)

CLIP_BOUND = 70000.0
LOSS_SCALE = 1024.0
BETA_ONE = 0.9
BETA_TWO = 0.999
FIRST_FIX = 1.0 - 0.9**50
SECOND_FIX = 1.0 - 0.999**50
ADAM_EPS = 1e-08
NORM_EPS = 1e-05

F32 = jnp.float32
BF16 = jnp.bfloat16


def dot_nn(a, b):
    return jnp.dot(a, b, preferred_element_type=F32)


def dot_nt(a, b):
    return lax.dot_general(a, b, (((1,), (1,)), ((), ())), preferred_element_type=F32)


def chain_kernel(
    scal,
    tokens,
    normed0,
    gout3,
    gram_n0,
    gram_g3,
    inv0,
    gains,
    own_col,
    own_row,
    *rest,
):
    pieces = rest[: 2 * PIECES]
    (
        keep_out,
        give_out,
        ratio,
        wv,
        hs,
        nm,
        go,
        inner,
        act,
        gin,
        acc,
        acc2,
        joint,
        sq,
        keep,
        give,
        wsems,
        isems,
        osems,
    ) = rest[2 * PIECES :]
    rows, width = tokens.shape
    chunks = width // CHUNK
    me, core, at_x, at_z = scal[4], scal[5], scal[6], scal[7]

    def chip_of(role, first, second):
        along_x = jnp.where(role == 0, first, second)
        along_z = jnp.where(role == 0, second, first)
        return lax.rem(at_x + along_x + RING, RING) * RING + lax.rem(at_z + along_z + RING, RING)

    def start_loads(section, which):
        slot = scal[section]
        for mine in range(2):

            @pl.when((core == which) == (mine == 1))
            def _(mine=mine):
                held = pieces[:PIECES] if mine else pieces[PIECES:]
                for index, (far, lo, hi) in enumerate(LAYOUT):
                    for near in range(lo, hi):
                        chip = chip_of(which, -near, -far)
                        pltpu.make_async_copy(
                            held[index].at[near - lo, slot],
                            wv.at[2 * section + which, pl.ds(chip * 256, 256), :],
                            wsems.at[2 * section + which],
                        ).start()

    def wait_load(section, which):
        whole = wv.at[2 * section + which]
        pltpu.make_async_copy(whole, whole, wsems.at[2 * section + which]).wait()

    start_loads(0, 0)
    first_inputs = [
        pltpu.make_async_copy(normed0, nm.at[0], isems.at[0]),
        pltpu.make_async_copy(tokens, hs.at[0], isems.at[1]),
        pltpu.make_async_copy(gout3, go.at[SECTIONS - 1], isems.at[2]),
    ]
    first_inputs[0].start()
    start_loads(0, 1)
    first_inputs[1].start()
    for section in range(1, SECTIONS):
        start_loads(section, 0)
        start_loads(section, 1)
    first_inputs[2].start()

    def cols(i):
        return pl.ds(pl.multiple_of(i * CHUNK, CHUNK), CHUNK)

    def each(body):
        def step(i, carry):
            body(cols(i))
            return carry

        lax.fori_loop(0, chunks, step, 0)

    inv = inv0[...]
    invs = [inv]
    for s in range(SECTIONS):
        wait_load(s, 0)
        slot = scal[s]
        if s == 0:
            first_inputs[0].wait()
            value = dot_nn(nm[0], wv[0])
        else:
            acc[...] = jnp.zeros_like(acc)
            acc2[...] = jnp.zeros_like(acc2)

            def norm_step(c, s=s, inv=inv, slot=slot):
                n = (hs[s, :, c].astype(F32) * inv * gains[slot, :, c]).astype(BF16)
                nm[s, :, c] = n
                acc[...] += dot_nn(n, wv[2 * s, c, :])
                acc2[...] += dot_nt(n, n)

            each(norm_step)
            value = acc[...]
            joint[s] = acc2[...]
        inner[s] = value
        active = (value * jax.nn.sigmoid(value)).astype(BF16)
        act[s] = active
        wait_load(s, 1)
        if s < SECTIONS - 1:
            if s == 0:
                first_inputs[1].wait()
            sq[...] = jnp.zeros_like(sq)

            def up_step(c, s=s, active=active):
                old = hs[s, :, c]
                new = (old.astype(F32) + dot_nt(active, wv[2 * s + 1, c, :])).astype(BF16)
                hs[s + 1, :, c] = new
                wide = new.astype(F32)
                wide = wide * wide
                part = wide[:, :128]
                for k in range(1, CHUNK // 128):
                    part = part + wide[:, 128 * k : 128 * (k + 1)]
                sq[...] += part

            each(up_step)
            mean = jnp.sum(sq[...], axis=-1, keepdims=True) * (1.0 / width)
            inv = lax.rsqrt(mean + NORM_EPS)
            invs.append(inv)

    total = jnp.zeros((rows, rows), F32)
    for s in reversed(range(SECTIONS)):
        if s == SECTIONS - 1:
            first_inputs[2].wait()
            gact = dot_nn(go[s], wv[2 * s + 1])
            gram_g = gram_g3[...]
        else:
            gact = acc[...]
            gram_g = acc2[...]
        value = inner[s]
        sig = jax.nn.sigmoid(value)
        gi = (gact * sig * (1.0 + value * (1.0 - sig))).astype(BF16)
        gin[s] = gi
        gram_n = gram_n0[...] if s == 0 else joint[s]
        total = total + gram_n * dot_nt(gi, gi) + dot_nt(act[s], act[s]) * gram_g
        if s > 0:
            inv = invs[s]
            proj = jnp.sum(gi.astype(F32) * value, axis=-1, keepdims=True) * (1.0 / width)
            coef = inv * inv * proj
            slot = scal[s]
            acc[...] = jnp.zeros_like(acc)
            acc2[...] = jnp.zeros_like(acc2)

            def back_step(c, s=s, inv=inv, coef=coef, gi=gi, slot=slot):
                gn = dot_nt(gi, wv[2 * s, c, :])
                above = go[s, :, c]
                g = (
                    above.astype(F32)
                    + inv * (gn * gains[slot, :, c])
                    - hs[s, :, c].astype(F32) * coef
                ).astype(BF16)
                go[s - 1, :, c] = g
                acc[...] += dot_nn(g, wv[2 * s - 1, c, :])
                acc2[...] += dot_nt(g, g)

            each(back_step)

    factor = jnp.zeros((rows, 1), F32)
    lane = lax.broadcasted_iota(jnp.int32, (1, 128), 1)
    report = jnp.zeros((1, 128), F32)
    for u in range(USERS_DEV):
        column = own_col[:, u : u + 1]
        part = jnp.sum(total * own_row[u : u + 1, :], axis=1, keepdims=True) * column
        norm = jnp.sqrt(jnp.sum(part, axis=0, keepdims=True))
        factor = factor + column * (LOSS_SCALE / jnp.maximum(norm, CLIP_BOUND))
        report = jnp.where(lane == u, norm * (1.0 / CLIP_BOUND), report)
    ratio[...] = jnp.broadcast_to(report, ratio.shape)

    wi = jnp.transpose(gin[me].astype(F32) * factor).astype(BF16)
    wa = jnp.transpose(act[me].astype(F32) * factor).astype(BF16)

    def emit(side):
        def step(index, carry):
            first, second = lax.div(index, RING), lax.rem(index, RING)
            for which in range(2):
                c = pl.ds(pl.multiple_of(chip_of(which, first, second) * 256, 256), 256)
                value = dot_nn((wi, wa)[which], (nm, go)[which][me, :, c])
                if which == side:
                    keep[first, second] = value
                else:
                    give[first, second] = value.astype(BF16)
            return carry

        for first in range(RING):
            lax.fori_loop(first * RING, (first + 1) * RING, step, 0)
            pltpu.make_async_copy(keep.at[first], keep_out.at[first], osems.at[first]).start()
            pltpu.make_async_copy(
                give.at[first], give_out.at[first], osems.at[RING + first]
            ).start()

    @pl.when(core == 0)
    def _():
        emit(0)

    @pl.when(core == 1)
    def _():
        emit(1)

    for first in range(RING):
        pltpu.make_async_copy(keep.at[first], keep_out.at[first], osems.at[first]).wait()
        pltpu.make_async_copy(give.at[first], give_out.at[first], osems.at[RING + first]).wait()


def run_chain(
    scal, tokens, normed0, gout3, gram_n0, gram_g3, inv0, gains, own_col, own_row, pieces
):
    rows, width = tokens.shape
    inner_width = pieces[0].shape[-1]
    vmem = pl.BlockSpec(memory_space=pltpu.VMEM)
    hbm = pl.BlockSpec(memory_space=pl.ANY)
    blocks = (RING, RING, inner_width, 256)
    wide = pltpu.VMEM((SECTIONS, rows, width), BF16)
    return pl.pallas_call(
        chain_kernel,
        out_shape=(
            jax.ShapeDtypeStruct(blocks, F32),
            jax.ShapeDtypeStruct(blocks, BF16),
            jax.ShapeDtypeStruct((8, 128), F32),
        ),
        in_specs=[pl.BlockSpec(memory_space=pltpu.SMEM)]
        + [hbm] * 3
        + [vmem] * 6
        + [hbm] * len(pieces),
        out_specs=(hbm, hbm, vmem),
        scratch_shapes=[
            pltpu.VMEM((2 * SECTIONS, width, inner_width), BF16),
            wide,
            wide,
            wide,
            pltpu.VMEM((SECTIONS, rows, inner_width), F32),
            pltpu.VMEM((SECTIONS, rows, inner_width), BF16),
            pltpu.VMEM((SECTIONS, rows, inner_width), BF16),
            pltpu.VMEM((rows, inner_width), F32),
            pltpu.VMEM((rows, rows), F32),
            pltpu.VMEM((SECTIONS, rows, rows), F32),
            pltpu.VMEM((rows, 128), F32),
            pltpu.VMEM(blocks, F32),
            pltpu.VMEM(blocks, BF16),
            pltpu.SemaphoreType.DMA((2 * SECTIONS,)),
            pltpu.SemaphoreType.DMA((3,)),
            pltpu.SemaphoreType.DMA((2 * RING,)),
        ],
        compiler_params=pltpu.CompilerParams(vmem_limit_bytes=60 * 1024 * 1024),
        name="chain",
    )(scal, tokens, normed0, gout3, gram_n0, gram_g3, inv0, gains, own_col, own_row, *pieces)


def moved(value, axes, shift):
    pairs = []
    for x in range(RING):
        for z in range(RING):
            for core in range(2):
                to = [x, z]
                if axes is not None:
                    to[axes[core] - 1] = (to[axes[core] - 1] + shift) % RING
                target = core if axes is not None else 1 - core
                pairs.append(((x * RING + z) * 2 + core, (to[0] * RING + to[1]) * 2 + target))
    return lax.ppermute(value, "dp", pairs)


def on_device(
    tokens, cotangent, lengths, seq_user, norm_gains, weights, first_moment, second_moment
):
    section_index = lax.axis_index("section")
    dp_index = lax.axis_index("dp")
    core = dp_index % 2
    at_x, at_z = dp_index // (2 * RING), (dp_index // 2) % RING
    tok_rows, model_width = tokens.shape
    rows = weights.shape[1]
    width = weights.shape[3]
    on_zero = core == 0
    near_axes, far_axes = (1, 2), (2, 1)

    shard = weights[0].astype(BF16)
    down, up = shard[:, 0, :], shard[:, 1, :]
    partner = moved(jnp.where(on_zero, up, down), None, 0)
    own = jnp.where(on_zero, down, up)
    gain = norm_gains[0]
    high = lax.reduce_precision(gain, 8, 7)
    middle = lax.reduce_precision(gain - high, 8, 7)
    low = gain - high - middle
    digits = jnp.stack([high, middle, low]).astype(BF16).reshape(-1, width)
    payload = jnp.concatenate(
        [jnp.where(on_zero, own, partner), jnp.where(on_zero, partner, own), digits], axis=0
    )
    held = [payload]
    for shift in (1, 3, 2):
        pairs = [(s, (s + shift) % SECTIONS) for s in range(SECTIONS)]
        held.append(lax.ppermute(payload, "section", pairs))
    held = [held[0], held[1], held[3], held[2]]
    column = jnp.stack([piece[: 2 * rows] for piece in held])
    got = [column] + [moved(column, near_axes, shift) for shift in (1, 3, 2)]
    plane = jnp.stack([got[0], got[1], got[3], got[2]])
    after = moved(plane, far_axes, 1)
    before = moved(plane, far_axes, 3)
    across_low = moved(after[:2], far_axes, 1)
    across_high = moved(before[2:], far_axes, 3)
    pieces = [plane, after, before, across_low, across_high]
    pieces = pieces + [moved(piece, None, 0) for piece in pieces]
    gains = jnp.stack(
        [
            jnp.sum(piece[2 * rows :].astype(F32).reshape(3, model_width), axis=0, keepdims=True)
            for piece in held
        ]
    )
    slots = (section_index - jnp.arange(SECTIONS)) % SECTIONS
    scal = jnp.concatenate([slots, jnp.stack([section_index, core, at_x, at_z])])
    scal = scal.astype(jnp.int32)

    positions = jnp.arange(tok_rows) % SEQLEN
    usable = positions < jnp.repeat(lengths, SEQLEN)
    token_user = jnp.repeat(seq_user - dp_index * USERS_DEV, SEQLEN)
    own_row = (
        (token_user[None, :] == jnp.arange(8)[:, None])
        & usable[None, :]
        & (jnp.arange(8) < USERS_DEV)[:, None]
    ).astype(F32)
    own_col = (
        (token_user[:, None] == jnp.arange(128)[None, :])
        & usable[:, None]
        & (jnp.arange(128) < USERS_DEV)[None, :]
    ).astype(F32)
    widened = tokens.astype(F32)
    inv0 = lax.rsqrt(jnp.mean(widened * widened, axis=-1, keepdims=True) + NORM_EPS)
    gain0 = lax.dynamic_index_in_dim(gains, slots[0], 0, keepdims=False)
    normed0 = (widened * inv0 * gain0).astype(BF16)
    gout3 = cotangent * usable[:, None].astype(BF16)
    keep, give, ratio = run_chain(
        scal,
        tokens,
        normed0,
        gout3,
        dot_nt(normed0, normed0),
        dot_nt(gout3, gout3),
        inv0,
        gains,
        own_col,
        own_row,
        pieces,
    )
    paired = (keep + moved(give, None, 0).astype(F32)).astype(BF16)
    parts = [moved(paired[shift], near_axes, shift) for shift in (1, 3, 2)]
    line = paired[0].astype(F32) + sum(part.astype(F32) for part in parts)
    line = line.astype(BF16)
    parts = [moved(line[shift], far_axes, shift) for shift in (1, 3, 2)]
    block = line[0].astype(F32) + sum(part.astype(F32) for part in parts)
    left, right = block[:, :rows], block[:, rows:]
    other = moved(jnp.where(on_zero, right, left), None, 0)
    mine = jnp.where(on_zero, left, right)
    gradient = jnp.stack(
        [jnp.where(on_zero, mine, other).T, jnp.where(on_zero, other, mine).T], axis=1
    )
    moment_one = BETA_ONE * first_moment[0] + (1.0 - BETA_ONE) * gradient
    moment_two = BETA_TWO * second_moment[0] + (1.0 - BETA_TWO) * gradient * gradient
    direction = moment_one / FIRST_FIX / (jnp.sqrt(moment_two / SECOND_FIX) + ADAM_EPS)
    return (moment_one[None], moment_two[None], direction[None], ratio[0, :USERS_DEV])


def solution(mesh):
    return jax.shard_map(
        on_device,
        mesh=mesh,
        in_specs=(
            P("dp", None),
            P("dp", None),
            P("dp"),
            P("dp"),
            P("section", None),
            P("section", "dp", None, None),
            P("section", "dp", None, None),
            P("section", "dp", None, None),
        ),
        out_specs=(
            P("section", "dp", None, None),
            P("section", "dp", None, None),
            P("section", "dp", None, None),
            P("dp"),
        ),
        check_vma=False,
    )
```

```python
import functools

import jax
import jax.numpy as jnp
from jax import lax
from jax.experimental import pallas as pl
from jax.experimental.pallas import tpu as pltpu
from jax.sharding import PartitionSpec as P

SEQLEN = 64
USERS_DEV = 2
SECTIONS = 4
CHUNK = 512
RING = 4
PIECES = RING * RING

CLIP_BOUND = 70000.0
LOSS_SCALE = 1024.0
BETA_ONE = 0.9
BETA_TWO = 0.999
FIRST_FIX = 1.0 - 0.9**50
SECOND_FIX = 1.0 - 0.999**50
ADAM_EPS = 1e-08
NORM_EPS = 1e-05

F32 = jnp.float32
BF16 = jnp.bfloat16


def dot_nn(a, b):
    return jnp.dot(a, b, preferred_element_type=F32)


def dot_nt(a, b):
    return lax.dot_general(a, b, (((1,), (1,)), ((), ())), preferred_element_type=F32)


def chain_kernel(
    scal,
    tokens,
    normed0,
    gout3,
    gram_n0,
    gram_g3,
    inv0,
    gains,
    own_col,
    own_row,
    *rest,
):
    pieces = rest[: 2 * PIECES]
    (
        give_out,
        left_out,
        right_out,
        ratio,
        wv,
        hs,
        rights,
        inner,
        act,
        gin,
        joint,
        sq,
        lefts,
        give,
        wsems,
        isems,
        osems,
    ) = rest[2 * PIECES :]
    nm, go = rights.at[:SECTIONS], rights.at[SECTIONS:]
    rows, width = tokens.shape
    chunks = width // CHUNK
    me, core, at_x, at_z = scal[4], scal[5], scal[6], scal[7]

    def chip_of(role, first, second):
        along_x = jnp.where(role == 0, first, second)
        along_z = jnp.where(role == 0, second, first)
        return lax.rem(at_x + along_x + RING, RING) * RING + lax.rem(at_z + along_z + RING, RING)

    def start_loads(section, which):
        slot = scal[section]
        for mine in range(2):

            @pl.when((core == which) == (mine == 1))
            def _(mine=mine):
                held = pieces[:PIECES] if mine else pieces[PIECES:]
                for index, piece in enumerate(held):
                    chip = chip_of(which, -(index % RING), -(index // RING))
                    pltpu.make_async_copy(
                        piece.at[slot],
                        wv.at[2 * section + which, pl.ds(chip * 256, 256), :],
                        wsems.at[2 * section + which],
                    ).start()

    def wait_load(section, which):
        whole = wv.at[2 * section + which]
        pltpu.make_async_copy(whole, whole, wsems.at[2 * section + which]).wait()

    start_loads(0, 0)
    first_inputs = [
        pltpu.make_async_copy(normed0, nm.at[0], isems.at[0]),
        pltpu.make_async_copy(tokens, hs.at[0], isems.at[1]),
        pltpu.make_async_copy(gout3, go.at[SECTIONS - 1], isems.at[2]),
    ]
    first_inputs[0].start()
    start_loads(0, 1)
    first_inputs[1].start()
    for section in range(1, SECTIONS):
        start_loads(section, 0)
        start_loads(section, 1)
    first_inputs[2].start()

    def cols(i):
        return pl.ds(pl.multiple_of(i * CHUNK, CHUNK), CHUNK)

    def each(body):
        def step(i, carry):
            body(cols(i))
            return carry

        lax.fori_loop(0, chunks, step, 0, unroll=True)

    inv = inv0[...]
    invs = [inv]
    for s in range(SECTIONS):
        wait_load(s, 0)
        slot = scal[s]
        if s == 0:
            first_inputs[0].wait()
            value = dot_nn(nm[0], wv[0])
        else:

            def norm_step(c, s=s, inv=inv, slot=slot):
                n = (hs[s, :, c].astype(F32) * inv * gains[slot, :, c]).astype(BF16)
                nm[s, :, c] = n

            each(norm_step)
            value = dot_nn(nm[s], wv[2 * s])
            joint[s] = dot_nt(nm[s], nm[s])
        inner[s] = value
        active = (value * jax.nn.sigmoid(value)).astype(BF16)
        act[s] = active
        wait_load(s, 1)
        if s < SECTIONS - 1:
            if s == 0:
                first_inputs[1].wait()
            sq[...] = jnp.zeros_like(sq)

            def up_step(c, s=s, active=active):
                old = hs[s, :, c]
                new = (old.astype(F32) + dot_nt(active, wv[2 * s + 1, c, :])).astype(BF16)
                hs[s + 1, :, c] = new
                wide = new.astype(F32)
                wide = wide * wide
                part = wide[:, :128]
                for k in range(1, CHUNK // 128):
                    part = part + wide[:, 128 * k : 128 * (k + 1)]
                sq[...] += part

            each(up_step)
            mean = jnp.sum(sq[...], axis=-1, keepdims=True) * (1.0 / width)
            inv = lax.rsqrt(mean + NORM_EPS)
            invs.append(inv)

    total = jnp.zeros((rows, rows), F32)
    for s in reversed(range(SECTIONS)):
        if s == SECTIONS - 1:
            first_inputs[2].wait()
            gact = dot_nn(go[s], wv[2 * s + 1])
            gram_g = gram_g3[...]
        else:
            gact = dot_nn(go[s], wv[2 * s + 1])
            gram_g = dot_nt(go[s], go[s])
        value = inner[s]
        sig = jax.nn.sigmoid(value)
        gi = (gact * sig * (1.0 + value * (1.0 - sig))).astype(BF16)
        gin[s] = gi
        gram_n = gram_n0[...] if s == 0 else joint[s]
        total = total + gram_n * dot_nt(gi, gi) + dot_nt(act[s], act[s]) * gram_g
        if s > 0:
            inv = invs[s]
            proj = jnp.sum(gi.astype(F32) * value, axis=-1, keepdims=True) * (1.0 / width)
            coef = inv * inv * proj
            slot = scal[s]

            def back_step(c, s=s, inv=inv, coef=coef, gi=gi, slot=slot):
                gn = dot_nt(gi, wv[2 * s, c, :])
                above = go[s, :, c]
                g = (
                    above.astype(F32)
                    + inv * (gn * gains[slot, :, c])
                    - hs[s, :, c].astype(F32) * coef
                ).astype(BF16)
                go[s - 1, :, c] = g

            each(back_step)

    factor = jnp.zeros((rows, 1), F32)
    lane = lax.broadcasted_iota(jnp.int32, (1, 128), 1)
    report = jnp.zeros((1, 128), F32)
    for u in range(USERS_DEV):
        column = own_col[:, u : u + 1]
        part = jnp.sum(total * own_row[u : u + 1, :], axis=1, keepdims=True) * column
        norm = jnp.sqrt(jnp.sum(part, axis=0, keepdims=True))
        factor = factor + column * (LOSS_SCALE / jnp.maximum(norm, CLIP_BOUND))
        report = jnp.where(lane == u, norm * (1.0 / CLIP_BOUND), report)
    ratio[...] = jnp.broadcast_to(report, ratio.shape)

    lefts[0] = jnp.transpose(gin[me].astype(F32) * factor).astype(BF16)
    lefts[1] = jnp.transpose(act[me].astype(F32) * factor).astype(BF16)

    other = 1 - core
    outs = [
        pltpu.make_async_copy(rights.at[core * SECTIONS + me], right_out, osems.at[RING]),
        pltpu.make_async_copy(lefts.at[core], left_out, osems.at[RING + 1]),
    ]
    for out in outs:
        out.start()
    for first in range(RING):
        for second in range(RING):
            c = pl.ds(pl.multiple_of(chip_of(other, first, second) * 256, 256), 256)
            value = dot_nn(lefts[other], rights[other * SECTIONS + me, :, c])
            give[first, second] = value.astype(BF16)
        out = pltpu.make_async_copy(give.at[first], give_out.at[first], osems.at[first])
        out.start()
        outs.append(out)
    for out in outs:
        out.wait()


def keep_kernel(scal, left, right, partner, *outs):
    core, at_x, at_z = scal[5], scal[6], scal[7]
    for first in range(RING):
        for second in range(RING):
            along_x = jnp.where(core == 0, first, second)
            along_z = jnp.where(core == 0, second, first)
            chip = lax.rem(at_x + along_x, RING) * RING + lax.rem(at_z + along_z, RING)
            c = pl.ds(pl.multiple_of(chip * 256, 256), 256)
            value = dot_nn(left[...], right[:, c]) + partner[first, second].astype(F32)
            outs[first][second] = value.astype(BF16)


def run_keep(scal, left, right, partner):
    vmem = pl.BlockSpec(memory_space=pltpu.VMEM)
    return pl.pallas_call(
        keep_kernel,
        out_shape=[jax.ShapeDtypeStruct(partner.shape[1:], BF16)] * RING,
        in_specs=[pl.BlockSpec(memory_space=pltpu.SMEM)] + [vmem] * 3,
        out_specs=[vmem] * RING,
        compiler_params=pltpu.CompilerParams(vmem_limit_bytes=24 * 1024 * 1024),
        name="keep",
    )(scal, left, right, partner)


def run_chain(
    scal, tokens, normed0, gout3, gram_n0, gram_g3, inv0, gains, own_col, own_row, pieces
):
    rows, width = tokens.shape
    inner_width = pieces[0].shape[-1]
    vmem = pl.BlockSpec(memory_space=pltpu.VMEM)
    hbm = pl.BlockSpec(memory_space=pl.ANY)
    blocks = (RING, RING, inner_width, 256)
    return pl.pallas_call(
        chain_kernel,
        out_shape=(
            jax.ShapeDtypeStruct(blocks, BF16),
            jax.ShapeDtypeStruct((rows, inner_width), BF16),
            jax.ShapeDtypeStruct((rows, width), BF16),
            jax.ShapeDtypeStruct((8, 128), F32),
        ),
        in_specs=[pl.BlockSpec(memory_space=pltpu.SMEM)]
        + [hbm] * 3
        + [vmem] * 6
        + [hbm] * len(pieces),
        out_specs=(hbm, hbm, hbm, vmem),
        scratch_shapes=[
            pltpu.VMEM((2 * SECTIONS, width, inner_width), BF16),
            pltpu.VMEM((SECTIONS, rows, width), BF16),
            pltpu.VMEM((2 * SECTIONS, rows, width), BF16),
            pltpu.VMEM((SECTIONS, rows, inner_width), F32),
            pltpu.VMEM((SECTIONS, rows, inner_width), BF16),
            pltpu.VMEM((SECTIONS, rows, inner_width), BF16),
            pltpu.VMEM((SECTIONS, rows, rows), F32),
            pltpu.VMEM((rows, 128), F32),
            pltpu.VMEM((2, rows, inner_width), BF16),
            pltpu.VMEM(blocks, BF16),
            pltpu.SemaphoreType.DMA((2 * SECTIONS,)),
            pltpu.SemaphoreType.DMA((3,)),
            pltpu.SemaphoreType.DMA((RING + 2,)),
        ],
        compiler_params=pltpu.CompilerParams(vmem_limit_bytes=60 * 1024 * 1024),
        name="chain",
    )(scal, tokens, normed0, gout3, gram_n0, gram_g3, inv0, gains, own_col, own_row, *pieces)


def moved(value, axes, shift):
    pairs = []
    for x in range(RING):
        for z in range(RING):
            for core in range(2):
                to = [x, z]
                if axes is not None:
                    to[axes[core] - 1] = (to[axes[core] - 1] + shift) % RING
                target = core if axes is not None else 1 - core
                pairs.append(((x * RING + z) * 2 + core, (to[0] * RING + to[1]) * 2 + target))
    return lax.ppermute(value, "dp", pairs)


def on_device(
    tokens, cotangent, lengths, seq_user, norm_gains, weights, first_moment, second_moment
):
    section_index = lax.axis_index("section")
    dp_index = lax.axis_index("dp")
    core = dp_index % 2
    at_x, at_z = dp_index // (2 * RING), (dp_index // 2) % RING
    tok_rows, model_width = tokens.shape
    rows = weights.shape[1]
    width = weights.shape[3]
    on_zero = core == 0
    near_axes, far_axes = (1, 2), (2, 1)

    shard = weights[0].astype(BF16)
    down, up = shard[:, 0, :], shard[:, 1, :]
    partner = moved(jnp.where(on_zero, up, down), None, 0)
    own = jnp.where(on_zero, down, up)
    gain = norm_gains[0]
    high = lax.reduce_precision(gain, 8, 7)
    middle = lax.reduce_precision(gain - high, 8, 7)
    low = gain - high - middle
    digits = jnp.stack([high, middle, low]).astype(BF16).reshape(-1, width)
    payload = jnp.concatenate(
        [jnp.where(on_zero, own, partner), jnp.where(on_zero, partner, own), digits], axis=0
    )
    held = [payload]
    for shift in (2, 1, 3):
        pairs = [(s, (s + shift) % SECTIONS) for s in range(SECTIONS)]
        held.append(lax.ppermute(payload, "section", pairs))
    held = [held[0], held[2], held[1], held[3]]
    column = jnp.stack([piece[: 2 * rows] for piece in held])
    gains = jnp.stack(
        [
            jnp.sum(piece[2 * rows :].astype(F32).reshape(3, model_width), axis=0, keepdims=True)
            for piece in held
        ]
    )
    slots = (section_index - jnp.arange(SECTIONS)) % SECTIONS
    scal = jnp.concatenate([slots, jnp.stack([section_index, core, at_x, at_z])])
    scal = scal.astype(jnp.int32)

    positions = jnp.arange(tok_rows) % SEQLEN
    usable = positions < jnp.repeat(lengths, SEQLEN)
    token_user = jnp.repeat(seq_user - dp_index * USERS_DEV, SEQLEN)
    own_row = (
        (token_user[None, :] == jnp.arange(8)[:, None])
        & usable[None, :]
        & (jnp.arange(8) < USERS_DEV)[:, None]
    ).astype(F32)
    own_col = (
        (token_user[:, None] == jnp.arange(128)[None, :])
        & usable[:, None]
        & (jnp.arange(128) < USERS_DEV)[None, :]
    ).astype(F32)
    widened = tokens.astype(F32)
    inv0 = lax.rsqrt(jnp.mean(widened * widened, axis=-1, keepdims=True) + NORM_EPS)
    gain0 = lax.dynamic_index_in_dim(gains, slots[0], 0, keepdims=False)
    normed0 = (widened * inv0 * gain0).astype(BF16)
    gout3 = cotangent * usable[:, None].astype(BF16)
    gram_n0, gram_g3 = dot_nt(normed0, normed0), dot_nt(gout3, gout3)
    near = [column] + [moved(column, near_axes, shift) for shift in (2, 1, 3)]
    near = [near[0], near[2], near[1], near[3]]
    near[1], normed0, gout3, gram_n0, gram_g3 = lax.optimization_barrier(
        (near[1], normed0, gout3, gram_n0, gram_g3)
    )
    order = (0, 1, 3, 2)
    after = {k: moved(near[k], far_axes, 1) for k in order}
    before = {k: moved(near[k], far_axes, 3) for k in order}
    across = {
        k: moved(after[k], far_axes, 1) if k < 2 else moved(before[k], far_axes, 3) for k in order
    }
    pieces = [line[k] for line in (near, after, across, before) for k in range(RING)]
    pieces = pieces + [moved(piece, None, 0) for piece in pieces]
    give, left, right, ratio = run_chain(
        scal,
        tokens,
        normed0,
        gout3,
        gram_n0,
        gram_g3,
        inv0,
        gains,
        own_col,
        own_row,
        pieces,
    )
    paired = run_keep(scal, left, right, moved(give, None, 0))
    parts = [moved(paired[shift], near_axes, shift) for shift in (2, 1, 3)]
    line = paired[0].astype(F32) + sum(part.astype(F32) for part in parts)
    line = line.astype(BF16)
    parts = [moved(line[shift], far_axes, shift) for shift in (2, 1, 3)]
    block = line[0].astype(F32) + sum(part.astype(F32) for part in parts)
    left, right = block[:, :rows], block[:, rows:]
    other = moved(jnp.where(on_zero, right, left), None, 0)
    mine = jnp.where(on_zero, left, right)
    gradient = jnp.stack(
        [jnp.where(on_zero, mine, other).T, jnp.where(on_zero, other, mine).T], axis=1
    )
    moment_one = BETA_ONE * first_moment[0] + (1.0 - BETA_ONE) * gradient
    moment_two = BETA_TWO * second_moment[0] + (1.0 - BETA_TWO) * gradient * gradient
    direction = moment_one / FIRST_FIX / (jnp.sqrt(moment_two / SECOND_FIX) + ADAM_EPS)
    return (moment_one[None], moment_two[None], direction[None], ratio[0, :USERS_DEV])


def solution(mesh):
    return jax.shard_map(
        on_device,
        mesh=mesh,
        in_specs=(
            P("dp", None),
            P("dp", None),
            P("dp"),
            P("dp"),
            P("section", None),
            P("section", "dp", None, None),
            P("section", "dp", None, None),
            P("section", "dp", None, None),
        ),
        out_specs=(
            P("section", "dp", None, None),
            P("section", "dp", None, None),
            P("section", "dp", None, None),
            P("dp"),
        ),
        check_vma=False,
    )
```

```python
import jax
import jax.numpy as jnp
from jax import lax
from jax.experimental import pallas as pl
from jax.experimental.pallas import tpu as pltpu
from jax.sharding import PartitionSpec as P


SEQLEN = 64
USERS_DEV = 2
SECTIONS = 4
CHUNK = 512
RING = 4
PIECES = RING * RING

CLIP_BOUND = 70000.0
LOSS_SCALE = 1024.0
BETA_ONE = 0.9
BETA_TWO = 0.999
FIRST_FIX = 1.0 - 0.9**50
SECOND_FIX = 1.0 - 0.999**50
ADAM_EPS = 1e-08
NORM_EPS = 1e-05

F32 = jnp.float32
BF16 = jnp.bfloat16


def dot_nn(a, b):
    return jnp.dot(a, b, preferred_element_type=F32)


def dot_nt(a, b):
    return lax.dot_general(a, b, (((1,), (1,)), ((), ())), preferred_element_type=F32)


def chain_kernel(
    scal,
    tokens,
    normed0,
    gout3,
    gram_n0,
    gram_g3,
    inv0,
    gains,
    own_col,
    own_row,
    *rest,
):
    pieces = rest[: 2 * PIECES]
    (
        give_out,
        left_out,
        right_out,
        ratio,
        wv,
        hs,
        rights,
        inner,
        act,
        gin,
        joint,
        sq,
        lefts,
        give,
        wsems,
        isems,
        osems,
    ) = rest[2 * PIECES :]
    nm, go = rights.at[:SECTIONS], rights.at[SECTIONS:]
    rows, width = tokens.shape
    chunks = width // CHUNK
    me, core, at_x, at_z = scal[4], scal[5], scal[6], scal[7]

    def chip_of(role, first, second):
        along_x = jnp.where(role == 0, first, second)
        along_z = jnp.where(role == 0, second, first)
        return lax.rem(at_x + along_x + RING, RING) * RING + lax.rem(at_z + along_z + RING, RING)

    def start_loads(section, which):
        slot = scal[section]
        for mine in range(2):

            @pl.when((core == which) == (mine == 1))
            def _(mine=mine):
                held = pieces[:PIECES] if mine else pieces[PIECES:]
                for index, piece in enumerate(held):
                    chip = chip_of(which, -(index % RING), -(index // RING))
                    pltpu.make_async_copy(
                        piece.at[slot],
                        wv.at[2 * section + which, pl.ds(chip * 256, 256), :],
                        wsems.at[2 * section + which],
                    ).start()

    def wait_load(section, which):
        whole = wv.at[2 * section + which]
        pltpu.make_async_copy(whole, whole, wsems.at[2 * section + which]).wait()

    start_loads(0, 0)
    first_inputs = [
        pltpu.make_async_copy(normed0, nm.at[0], isems.at[0]),
        pltpu.make_async_copy(tokens, hs.at[0], isems.at[1]),
        pltpu.make_async_copy(gout3, go.at[SECTIONS - 1], isems.at[2]),
    ]
    first_inputs[0].start()
    start_loads(0, 1)
    first_inputs[1].start()
    for section in range(1, SECTIONS):
        start_loads(section, 0)
        start_loads(section, 1)
    first_inputs[2].start()

    def cols(i):
        return pl.ds(pl.multiple_of(i * CHUNK, CHUNK), CHUNK)

    def each(body):
        def step(i, carry):
            body(cols(i))
            return carry

        lax.fori_loop(0, chunks, step, 0, unroll=True)

    inv = inv0[...]
    invs = [inv]
    for s in range(SECTIONS):
        wait_load(s, 0)
        slot = scal[s]
        if s == 0:
            first_inputs[0].wait()
            value = dot_nn(nm[0], wv[0])
        else:

            def norm_step(c, s=s, inv=inv, slot=slot):
                n = (hs[s, :, c].astype(F32) * inv * gains[slot, :, c]).astype(BF16)
                nm[s, :, c] = n

            each(norm_step)
            value = dot_nn(nm[s], wv[2 * s])
            joint[s] = dot_nt(nm[s], nm[s])
        inner[s] = value
        active = (value * jax.nn.sigmoid(value)).astype(BF16)
        act[s] = active
        wait_load(s, 1)
        if s < SECTIONS - 1:
            if s == 0:
                first_inputs[1].wait()
            sq[...] = jnp.zeros_like(sq)

            def up_step(c, s=s, active=active):
                old = hs[s, :, c]
                new = (old.astype(F32) + dot_nt(active, wv[2 * s + 1, c, :])).astype(BF16)
                hs[s + 1, :, c] = new
                wide = new.astype(F32)
                wide = wide * wide
                part = wide[:, :128]
                for k in range(1, CHUNK // 128):
                    part = part + wide[:, 128 * k : 128 * (k + 1)]
                sq[...] += part

            each(up_step)
            mean = jnp.sum(sq[...], axis=-1, keepdims=True) * (1.0 / width)
            inv = lax.rsqrt(mean + NORM_EPS)
            invs.append(inv)

    total = jnp.zeros((rows, rows), F32)
    for s in reversed(range(SECTIONS)):
        if s == SECTIONS - 1:
            first_inputs[2].wait()
            gact = dot_nn(go[s], wv[2 * s + 1])
            gram_g = gram_g3[...]
        else:
            gact = dot_nn(go[s], wv[2 * s + 1])
            gram_g = dot_nt(go[s], go[s])
        value = inner[s]
        sig = jax.nn.sigmoid(value)
        gi = (gact * sig * (1.0 + value * (1.0 - sig))).astype(BF16)
        gin[s] = gi
        gram_n = gram_n0[...] if s == 0 else joint[s]
        total = total + gram_n * dot_nt(gi, gi) + dot_nt(act[s], act[s]) * gram_g
        if s > 0:
            inv = invs[s]
            proj = jnp.sum(gi.astype(F32) * value, axis=-1, keepdims=True) * (1.0 / width)
            coef = inv * inv * proj
            slot = scal[s]

            def back_step(c, s=s, inv=inv, coef=coef, gi=gi, slot=slot):
                gn = dot_nt(gi, wv[2 * s, c, :])
                above = go[s, :, c]
                g = (
                    above.astype(F32)
                    + inv * (gn * gains[slot, :, c])
                    - hs[s, :, c].astype(F32) * coef
                ).astype(BF16)
                go[s - 1, :, c] = g

            each(back_step)

    factor = jnp.zeros((rows, 1), F32)
    lane = lax.broadcasted_iota(jnp.int32, (1, 128), 1)
    report = jnp.zeros((1, 128), F32)
    for u in range(USERS_DEV):
        column = own_col[:, u : u + 1]
        part = jnp.sum(total * own_row[u : u + 1, :], axis=1, keepdims=True) * column
        norm = jnp.sqrt(jnp.sum(part, axis=0, keepdims=True))
        factor = factor + column * (LOSS_SCALE / jnp.maximum(norm, CLIP_BOUND))
        report = jnp.where(lane == u, norm * (1.0 / CLIP_BOUND), report)
    ratio[...] = jnp.broadcast_to(report, ratio.shape)

    lefts[0] = jnp.transpose(gin[me].astype(F32) * factor).astype(BF16)
    lefts[1] = jnp.transpose(act[me].astype(F32) * factor).astype(BF16)

    other = 1 - core
    outs = [
        pltpu.make_async_copy(rights.at[core * SECTIONS + me], right_out, osems.at[RING]),
        pltpu.make_async_copy(lefts.at[core], left_out, osems.at[RING + 1]),
    ]
    for out in outs:
        out.start()

    def give_copy(first):
        return pltpu.make_async_copy(give.at[first], give_out.at[first], osems.at[first])

    def emit(first, carry):
        for second in range(RING):
            c = pl.ds(pl.multiple_of(chip_of(other, first, second) * 256, 256), 256)
            value = dot_nn(lefts[other], rights[other * SECTIONS + me, :, c])
            give[first, second] = value.astype(BF16)
        give_copy(first).start()
        return carry

    lax.fori_loop(0, RING, emit, 0)
    for out in outs + [give_copy(first) for first in range(RING)]:
        out.wait()


def keep_kernel(scal, left_in, right_in, partner_in, *rest):
    outs, (left, right, partner, paired, isems, osems) = rest[:RING], rest[RING:]
    core, at_x, at_z = scal[5], scal[6], scal[7]

    def chip(first, second):
        along_x = jnp.where(core == 0, first, second)
        along_z = jnp.where(core == 0, second, first)
        return lax.rem(at_x + along_x, RING) * RING + lax.rem(at_z + along_z, RING)

    left_copy = pltpu.make_async_copy(left_in, left, isems.at[0])
    left_copy.start()
    order = (2, 1, 3, 0)
    copies = {}
    for first in order:
        for second in range(RING):
            c = pl.ds(pl.multiple_of(chip(first, second) * 256, 256), 256)
            slot = first * RING + second
            copies[first, second] = pltpu.make_async_copy(
                right_in.at[:, c], right.at[slot], isems.at[1 + slot]
            )
            copies[first, second].start()
        copies[first] = pltpu.make_async_copy(
            partner_in.at[first], partner.at[first], isems.at[1 + RING * RING + first]
        )
        copies[first].start()
    left_copy.wait()
    sends = []
    for first in order:
        copies[first].wait()
        for second in range(RING):
            copies[first, second].wait()
            value = dot_nn(left[...], right[first * RING + second])
            value = value + partner[first, second].astype(F32)
            paired[first, second] = value.astype(BF16)
        sends.append(pltpu.make_async_copy(paired.at[first], outs[first], osems.at[first]))
        sends[-1].start()
    for send in sends:
        send.wait()


def run_keep(scal, left, right, partner):
    hbm = pl.BlockSpec(memory_space=pl.ANY)
    return pl.pallas_call(
        keep_kernel,
        out_shape=[jax.ShapeDtypeStruct(partner.shape[1:], BF16)] * RING,
        in_specs=[pl.BlockSpec(memory_space=pltpu.SMEM)] + [hbm] * 3,
        out_specs=[hbm] * RING,
        scratch_shapes=[
            pltpu.VMEM(left.shape, BF16),
            pltpu.VMEM((RING * RING, right.shape[0], 256), BF16),
            pltpu.VMEM(partner.shape, BF16),
            pltpu.VMEM(partner.shape, BF16),
            pltpu.SemaphoreType.DMA((1 + RING * RING + RING,)),
            pltpu.SemaphoreType.DMA((RING,)),
        ],
        compiler_params=pltpu.CompilerParams(vmem_limit_bytes=24 * 1024 * 1024),
        name="keep",
    )(scal, left, right, partner)


def run_chain(
    scal, tokens, normed0, gout3, gram_n0, gram_g3, inv0, gains, own_col, own_row, pieces
):
    rows, width = tokens.shape
    inner_width = pieces[0].shape[-1]
    vmem = pl.BlockSpec(memory_space=pltpu.VMEM)
    hbm = pl.BlockSpec(memory_space=pl.ANY)
    blocks = (RING, RING, inner_width, 256)
    return pl.pallas_call(
        chain_kernel,
        out_shape=(
            jax.ShapeDtypeStruct(blocks, BF16),
            jax.ShapeDtypeStruct((rows, inner_width), BF16),
            jax.ShapeDtypeStruct((rows, width), BF16),
            jax.ShapeDtypeStruct((8, 128), F32),
        ),
        in_specs=[pl.BlockSpec(memory_space=pltpu.SMEM)]
        + [hbm] * 3
        + [vmem] * 6
        + [hbm] * len(pieces),
        out_specs=(hbm, hbm, hbm, vmem),
        scratch_shapes=[
            pltpu.VMEM((2 * SECTIONS, width, inner_width), BF16),
            pltpu.VMEM((SECTIONS, rows, width), BF16),
            pltpu.VMEM((2 * SECTIONS, rows, width), BF16),
            pltpu.VMEM((SECTIONS, rows, inner_width), F32),
            pltpu.VMEM((SECTIONS, rows, inner_width), BF16),
            pltpu.VMEM((SECTIONS, rows, inner_width), BF16),
            pltpu.VMEM((SECTIONS, rows, rows), F32),
            pltpu.VMEM((rows, 128), F32),
            pltpu.VMEM((2, rows, inner_width), BF16),
            pltpu.VMEM(blocks, BF16),
            pltpu.SemaphoreType.DMA((2 * SECTIONS,)),
            pltpu.SemaphoreType.DMA((3,)),
            pltpu.SemaphoreType.DMA((RING + 2,)),
        ],
        compiler_params=pltpu.CompilerParams(vmem_limit_bytes=60 * 1024 * 1024),
        name="chain",
    )(scal, tokens, normed0, gout3, gram_n0, gram_g3, inv0, gains, own_col, own_row, *pieces)


def moved(value, axes, shift):
    pairs = []
    for x in range(RING):
        for z in range(RING):
            for core in range(2):
                to = [x, z]
                if axes is not None:
                    to[axes[core] - 1] = (to[axes[core] - 1] + shift) % RING
                target = core if axes is not None else 1 - core
                pairs.append(((x * RING + z) * 2 + core, (to[0] * RING + to[1]) * 2 + target))
    return lax.ppermute(value, "dp", pairs)


def on_device(
    tokens, cotangent, lengths, seq_user, norm_gains, weights, first_moment, second_moment
):
    section_index = lax.axis_index("section")
    dp_index = lax.axis_index("dp")
    core = dp_index % 2
    at_x, at_z = dp_index // (2 * RING), (dp_index // 2) % RING
    tok_rows, model_width = tokens.shape
    rows = weights.shape[1]
    width = weights.shape[3]
    on_zero = core == 0
    near_axes, far_axes = (1, 2), (2, 1)

    shard = weights[0].astype(BF16)
    down, up = shard[:, 0, :], shard[:, 1, :]
    partner = moved(jnp.where(on_zero, up, down), None, 0)
    own = jnp.where(on_zero, down, up)
    gain = norm_gains[0]
    high = lax.reduce_precision(gain, 8, 7)
    middle = lax.reduce_precision(gain - high, 8, 7)
    low = gain - high - middle
    digits = jnp.stack([high, middle, low]).astype(BF16).reshape(-1, width)
    payload = jnp.concatenate(
        [jnp.where(on_zero, own, partner), jnp.where(on_zero, partner, own), digits], axis=0
    )
    held = [payload]
    for shift in (2, 1, 3):
        pairs = [(s, (s + shift) % SECTIONS) for s in range(SECTIONS)]
        held.append(lax.ppermute(payload, "section", pairs))
    held = [held[0], held[2], held[1], held[3]]
    column = jnp.stack([piece[: 2 * rows] for piece in held])
    column, cotangent = lax.optimization_barrier((column, cotangent))
    gains = jnp.stack(
        [
            jnp.sum(piece[2 * rows :].astype(F32).reshape(3, model_width), axis=0, keepdims=True)
            for piece in held
        ]
    )
    slots = (section_index - jnp.arange(SECTIONS)) % SECTIONS
    scal = jnp.concatenate([slots, jnp.stack([section_index, core, at_x, at_z])])
    scal = scal.astype(jnp.int32)

    positions = jnp.arange(tok_rows) % SEQLEN
    usable = positions < jnp.repeat(lengths, SEQLEN)
    token_user = jnp.repeat(seq_user - dp_index * USERS_DEV, SEQLEN)
    own_row = (
        (token_user[None, :] == jnp.arange(8)[:, None])
        & usable[None, :]
        & (jnp.arange(8) < USERS_DEV)[:, None]
    ).astype(F32)
    own_col = (
        (token_user[:, None] == jnp.arange(128)[None, :])
        & usable[:, None]
        & (jnp.arange(128) < USERS_DEV)[None, :]
    ).astype(F32)
    widened = tokens.astype(F32)
    inv0 = lax.rsqrt(jnp.mean(widened * widened, axis=-1, keepdims=True) + NORM_EPS)
    gain0 = lax.dynamic_index_in_dim(gains, slots[0], 0, keepdims=False)
    normed0 = (widened * inv0 * gain0).astype(BF16)
    gout3 = cotangent * usable[:, None].astype(BF16)
    gram_n0, gram_g3 = dot_nt(normed0, normed0), dot_nt(gout3, gout3)
    near = [column] + [moved(column, near_axes, shift) for shift in (1, 2, 3)]
    near[1], normed0, gout3, gram_n0, gram_g3, inv0, scal, own_row, own_col = (
        lax.optimization_barrier(
            (near[1], normed0, gout3, gram_n0, gram_g3, inv0, scal, own_row, own_col)
        )
    )
    after = [moved(near[k], far_axes, 1) for k in range(RING)]
    before = [moved(near[k], far_axes, 3) for k in range(RING)]
    across = [
        moved(after[k], far_axes, 1)
        if k < 2
        else moved(before[k], far_axes, 3)
        for k in range(RING)
    ]
    pieces = [line[k] for line in (near, after, across, before) for k in range(RING)]
    pieces = pieces + [moved(piece, None, 0) for piece in pieces]
    give, left, right, ratio = run_chain(
        scal,
        tokens,
        normed0,
        gout3,
        gram_n0,
        gram_g3,
        inv0,
        gains,
        own_col,
        own_row,
        pieces,
    )
    paired = run_keep(scal, left, right, moved(give, None, 0))
    parts = [moved(paired[shift], near_axes, shift) for shift in (2, 1, 3)]
    line = paired[0].astype(F32) + sum(part.astype(F32) for part in parts)
    line = line.astype(BF16)
    parts = [moved(line[shift], far_axes, shift) for shift in (2, 1, 3)]
    block = line[0].astype(F32) + sum(part.astype(F32) for part in parts)
    left, right = block[:, :rows], block[:, rows:]
    other = moved(jnp.where(on_zero, right, left), None, 0)
    mine = jnp.where(on_zero, left, right)
    gradient = jnp.stack(
        [jnp.where(on_zero, mine, other).T, jnp.where(on_zero, other, mine).T], axis=1
    )
    moment_one = BETA_ONE * first_moment[0] + (1.0 - BETA_ONE) * gradient
    moment_two = BETA_TWO * second_moment[0] + (1.0 - BETA_TWO) * gradient * gradient
    direction = moment_one / FIRST_FIX / (jnp.sqrt(moment_two / SECOND_FIX) + ADAM_EPS)
    return (moment_one[None], moment_two[None], direction[None], ratio[0, :USERS_DEV])


def solution(mesh):
    return jax.shard_map(
        on_device,
        mesh=mesh,
        in_specs=(
            P("dp", None),
            P("dp", None),
            P("dp"),
            P("dp"),
            P("section", None),
            P("section", "dp", None, None),
            P("section", "dp", None, None),
            P("section", "dp", None, None),
        ),
        out_specs=(
            P("section", "dp", None, None),
            P("section", "dp", None, None),
            P("section", "dp", None, None),
            P("dp"),
        ),
        check_vma=False,
    )
```

```python
import jax
import jax.numpy as jnp
from jax import lax
from jax.experimental import pallas as pl
from jax.experimental.pallas import tpu as pltpu
from jax.sharding import PartitionSpec as P


SEQLEN = 64
USERS_DEV = 2
SECTIONS = 4
CHUNK = 512
RING = 4
PIECES = RING * RING

CLIP_BOUND = 70000.0
LOSS_SCALE = 1024.0
BETA_ONE = 0.9
BETA_TWO = 0.999
FIRST_FIX = 1.0 - 0.9**50
SECOND_FIX = 1.0 - 0.999**50
ADAM_EPS = 1e-08
NORM_EPS = 1e-05

F32 = jnp.float32
BF16 = jnp.bfloat16


def dot_nn(a, b):
    return jnp.dot(a, b, preferred_element_type=F32)


def dot_nt(a, b):
    return lax.dot_general(a, b, (((1,), (1,)), ((), ())), preferred_element_type=F32)


def chain_kernel(
    scal,
    tokens,
    normed0,
    gout3,
    gram_n0,
    gram_g3,
    inv0,
    gains,
    own_col,
    own_row,
    *rest,
):
    pieces = rest[: 2 * PIECES]
    (
        ratio,
        wv,
        hs,
        rights,
        inner,
        act,
        gin,
        joint,
        sq,
        lefts,
        keep,
        give,
        wsems,
        isems,
        osems,
    ) = rest[2 * PIECES + 2 * RING :]
    keep_outs = rest[2 * PIECES : 2 * PIECES + RING]
    give_outs = rest[2 * PIECES + RING : 2 * PIECES + 2 * RING]
    nm, go = rights.at[:SECTIONS], rights.at[SECTIONS:]
    rows, width = tokens.shape
    chunks = width // CHUNK
    me, core, at_x, at_z = scal[4], scal[5], scal[6], scal[7]

    def chip_of(role, first, second):
        along_x = jnp.where(role == 0, first, second)
        along_z = jnp.where(role == 0, second, first)
        return lax.rem(at_x + along_x + RING, RING) * RING + lax.rem(at_z + along_z + RING, RING)

    def start_loads(section, which):
        slot = scal[section]
        for mine in range(2):

            @pl.when((core == which) == (mine == 1))
            def _(mine=mine):
                held = pieces[:PIECES] if mine else pieces[PIECES:]
                for index, piece in enumerate(held):
                    chip = chip_of(which, -(index % RING), -(index // RING))
                    pltpu.make_async_copy(
                        piece.at[slot],
                        wv.at[2 * section + which, pl.ds(chip * 256, 256), :],
                        wsems.at[2 * section + which],
                    ).start()

    def wait_load(section, which):
        whole = wv.at[2 * section + which]
        pltpu.make_async_copy(whole, whole, wsems.at[2 * section + which]).wait()

    start_loads(0, 0)
    first_inputs = [
        pltpu.make_async_copy(normed0, nm.at[0], isems.at[0]),
        pltpu.make_async_copy(tokens, hs.at[0], isems.at[1]),
        pltpu.make_async_copy(gout3, go.at[SECTIONS - 1], isems.at[2]),
    ]
    first_inputs[0].start()
    start_loads(0, 1)
    first_inputs[1].start()
    for section in range(1, SECTIONS):
        start_loads(section, 0)
        start_loads(section, 1)
    first_inputs[2].start()

    def cols(i):
        return pl.ds(pl.multiple_of(i * CHUNK, CHUNK), CHUNK)

    def each(body):
        def step(i, carry):
            body(cols(i))
            return carry

        lax.fori_loop(0, chunks, step, 0, unroll=True)

    inv = inv0[...]
    invs = [inv]
    for s in range(SECTIONS):
        wait_load(s, 0)
        slot = scal[s]
        if s == 0:
            first_inputs[0].wait()
            value = dot_nn(nm[0], wv[0])
        else:

            def norm_step(c, s=s, inv=inv, slot=slot):
                n = (hs[s, :, c].astype(F32) * inv * gains[slot, :, c]).astype(BF16)
                nm[s, :, c] = n

            each(norm_step)
            value = dot_nn(nm[s], wv[2 * s])
            joint[s] = dot_nt(nm[s], nm[s])
        inner[s] = value
        active = (value * jax.nn.sigmoid(value)).astype(BF16)
        act[s] = active
        wait_load(s, 1)
        if s < SECTIONS - 1:
            if s == 0:
                first_inputs[1].wait()
            sq[...] = jnp.zeros_like(sq)

            def up_step(c, s=s, active=active):
                old = hs[s, :, c]
                new = (old.astype(F32) + dot_nt(active, wv[2 * s + 1, c, :])).astype(BF16)
                hs[s + 1, :, c] = new
                wide = new.astype(F32)
                wide = wide * wide
                part = wide[:, :128]
                for k in range(1, CHUNK // 128):
                    part = part + wide[:, 128 * k : 128 * (k + 1)]
                sq[...] += part

            each(up_step)
            mean = jnp.sum(sq[...], axis=-1, keepdims=True) * (1.0 / width)
            inv = lax.rsqrt(mean + NORM_EPS)
            invs.append(inv)

    total = jnp.zeros((rows, rows), F32)
    for s in reversed(range(SECTIONS)):
        if s == SECTIONS - 1:
            first_inputs[2].wait()
            gact = dot_nn(go[s], wv[2 * s + 1])
            gram_g = gram_g3[...]
        else:
            gact = dot_nn(go[s], wv[2 * s + 1])
            gram_g = dot_nt(go[s], go[s])
        value = inner[s]
        sig = jax.nn.sigmoid(value)
        gi = (gact * sig * (1.0 + value * (1.0 - sig))).astype(BF16)
        gin[s] = gi
        gram_n = gram_n0[...] if s == 0 else joint[s]
        total = total + gram_n * dot_nt(gi, gi) + dot_nt(act[s], act[s]) * gram_g
        if s > 0:
            inv = invs[s]
            proj = jnp.sum(gi.astype(F32) * value, axis=-1, keepdims=True) * (1.0 / width)
            coef = inv * inv * proj
            slot = scal[s]

            def back_step(c, s=s, inv=inv, coef=coef, gi=gi, slot=slot):
                gn = dot_nt(gi, wv[2 * s, c, :])
                above = go[s, :, c]
                g = (
                    above.astype(F32)
                    + inv * (gn * gains[slot, :, c])
                    - hs[s, :, c].astype(F32) * coef
                ).astype(BF16)
                go[s - 1, :, c] = g

            each(back_step)

    factor = jnp.zeros((rows, 1), F32)
    lane = lax.broadcasted_iota(jnp.int32, (1, 128), 1)
    report = jnp.zeros((1, 128), F32)
    for u in range(USERS_DEV):
        column = own_col[:, u : u + 1]
        part = jnp.sum(total * own_row[u : u + 1, :], axis=1, keepdims=True) * column
        norm = jnp.sqrt(jnp.sum(part, axis=0, keepdims=True))
        factor = factor + column * (LOSS_SCALE / jnp.maximum(norm, CLIP_BOUND))
        report = jnp.where(lane == u, norm * (1.0 / CLIP_BOUND), report)
    ratio[...] = jnp.broadcast_to(report, ratio.shape)

    lefts[0] = jnp.transpose(gin[me].astype(F32) * factor).astype(BF16)
    lefts[1] = jnp.transpose(act[me].astype(F32) * factor).astype(BF16)

    other = 1 - core

    def emit(which, target):
        def step(first, carry):
            for second in range(RING):
                c = pl.ds(pl.multiple_of(chip_of(which, first, second) * 256, 256), 256)
                value = dot_nn(lefts[which], rights[which * SECTIONS + me, :, c])
                target[first, second] = value.astype(target.dtype)
            return carry

        lax.fori_loop(0, RING, step, 0)

    outs = []
    for base, which, source, targets in (
        (0, core, keep, keep_outs),
        (RING, other, give, give_outs),
    ):
        emit(which, source)
        for first in range(RING):
            outs.append(
                pltpu.make_async_copy(source.at[first], targets[first], osems.at[base + first])
            )
            outs[-1].start()
    for out in outs:
        out.wait()


def run_chain(
    scal, tokens, normed0, gout3, gram_n0, gram_g3, inv0, gains, own_col, own_row, pieces
):
    rows, width = tokens.shape
    inner_width = pieces[0].shape[-1]
    vmem = pl.BlockSpec(memory_space=pltpu.VMEM)
    hbm = pl.BlockSpec(memory_space=pl.ANY)
    blocks = (RING, RING, inner_width, 256)
    return pl.pallas_call(
        chain_kernel,
        out_shape=[jax.ShapeDtypeStruct(blocks[1:], F32)] * RING
        + [jax.ShapeDtypeStruct(blocks[1:], BF16)] * RING
        + [jax.ShapeDtypeStruct((8, 128), F32)],
        in_specs=[pl.BlockSpec(memory_space=pltpu.SMEM)]
        + [hbm] * 3
        + [vmem] * 6
        + [hbm] * len(pieces),
        out_specs=[hbm] * (2 * RING) + [vmem],
        scratch_shapes=[
            pltpu.VMEM((2 * SECTIONS, width, inner_width), BF16),
            pltpu.VMEM((SECTIONS, rows, width), BF16),
            pltpu.VMEM((2 * SECTIONS, rows, width), BF16),
            pltpu.VMEM((SECTIONS, rows, inner_width), F32),
            pltpu.VMEM((SECTIONS, rows, inner_width), BF16),
            pltpu.VMEM((SECTIONS, rows, inner_width), BF16),
            pltpu.VMEM((SECTIONS, rows, rows), F32),
            pltpu.VMEM((rows, 128), F32),
            pltpu.VMEM((2, rows, inner_width), BF16),
            pltpu.VMEM(blocks, F32),
            pltpu.VMEM(blocks, BF16),
            pltpu.SemaphoreType.DMA((2 * SECTIONS,)),
            pltpu.SemaphoreType.DMA((3,)),
            pltpu.SemaphoreType.DMA((2 * RING,)),
        ],
        compiler_params=pltpu.CompilerParams(vmem_limit_bytes=54 * 1024 * 1024),
        name="chain",
    )(scal, tokens, normed0, gout3, gram_n0, gram_g3, inv0, gains, own_col, own_row, *pieces)


def moved(value, axes, shift):
    pairs = []
    for x in range(RING):
        for z in range(RING):
            for core in range(2):
                to = [x, z]
                if axes is not None:
                    to[axes[core] - 1] = (to[axes[core] - 1] + shift) % RING
                target = core if axes is not None else 1 - core
                pairs.append(((x * RING + z) * 2 + core, (to[0] * RING + to[1]) * 2 + target))
    return lax.ppermute(value, "dp", pairs)


def on_device(
    tokens, cotangent, lengths, seq_user, norm_gains, weights, first_moment, second_moment
):
    section_index = lax.axis_index("section")
    dp_index = lax.axis_index("dp")
    core = dp_index % 2
    at_x, at_z = dp_index // (2 * RING), (dp_index // 2) % RING
    tok_rows, model_width = tokens.shape
    rows = weights.shape[1]
    width = weights.shape[3]
    on_zero = core == 0
    near_axes, far_axes = (1, 2), (2, 1)

    shard = weights[0].astype(BF16)
    down, up = shard[:, 0, :], shard[:, 1, :]
    partner = moved(jnp.where(on_zero, up, down), None, 0)
    own = jnp.where(on_zero, down, up)
    gain = norm_gains[0]
    high = lax.reduce_precision(gain, 8, 7)
    middle = lax.reduce_precision(gain - high, 8, 7)
    low = gain - high - middle
    digits = jnp.stack([high, middle, low]).astype(BF16).reshape(-1, width)
    payload = jnp.concatenate(
        [jnp.where(on_zero, own, partner), jnp.where(on_zero, partner, own), digits], axis=0
    )
    held = [payload]
    for shift in (2, 1, 3):
        pairs = [(s, (s + shift) % SECTIONS) for s in range(SECTIONS)]
        held.append(lax.ppermute(payload, "section", pairs))
    held = [held[0], held[2], held[1], held[3]]
    column = jnp.stack([piece[: 2 * rows] for piece in held])
    column, cotangent = lax.optimization_barrier((column, cotangent))
    gains = jnp.stack(
        [
            jnp.sum(piece[2 * rows :].astype(F32).reshape(3, model_width), axis=0, keepdims=True)
            for piece in held
        ]
    )
    slots = (section_index - jnp.arange(SECTIONS)) % SECTIONS
    scal = jnp.concatenate([slots, jnp.stack([section_index, core, at_x, at_z])])
    scal = scal.astype(jnp.int32)

    positions = jnp.arange(tok_rows) % SEQLEN
    usable = positions < jnp.repeat(lengths, SEQLEN)
    token_user = jnp.repeat(seq_user - dp_index * USERS_DEV, SEQLEN)
    own_row = (
        (token_user[None, :] == jnp.arange(8)[:, None])
        & usable[None, :]
        & (jnp.arange(8) < USERS_DEV)[:, None]
    ).astype(F32)
    own_col = (
        (token_user[:, None] == jnp.arange(128)[None, :])
        & usable[:, None]
        & (jnp.arange(128) < USERS_DEV)[None, :]
    ).astype(F32)
    widened = tokens.astype(F32)
    inv0 = lax.rsqrt(jnp.mean(widened * widened, axis=-1, keepdims=True) + NORM_EPS)
    gain0 = lax.dynamic_index_in_dim(gains, slots[0], 0, keepdims=False)
    normed0 = (widened * inv0 * gain0).astype(BF16)
    gout3 = cotangent * usable[:, None].astype(BF16)
    gram_n0, gram_g3 = dot_nt(normed0, normed0), dot_nt(gout3, gout3)
    near = [column] + [moved(column, near_axes, shift) for shift in (1, 2, 3)]
    near[2], normed0, gout3, gram_n0, gram_g3, inv0, scal, own_row, own_col = (
        lax.optimization_barrier(
            (near[2], normed0, gout3, gram_n0, gram_g3, inv0, scal, own_row, own_col)
        )
    )
    after = [moved(near[k], far_axes, 1) for k in range(RING)]
    before = [moved(near[k], far_axes, 3) for k in range(RING)]
    across = [
        moved(after[k], far_axes, 1)
        if k < 2
        else moved(before[k], far_axes, 3)
        for k in range(RING)
    ]
    pieces = [line[k] for line in (near, after, across, before) for k in range(RING)]
    pieces = pieces + [moved(piece, None, 0) for piece in pieces]
    results = run_chain(
        scal,
        tokens,
        normed0,
        gout3,
        gram_n0,
        gram_g3,
        inv0,
        gains,
        own_col,
        own_row,
        pieces,
    )
    keeps, gives, ratio = results[:RING], results[RING : 2 * RING], results[-1][0, :USERS_DEV]
    paired = [None] * RING
    for first in (2, 1, 3, 0):
        partner = moved(gives[first], None, 0)
        paired[first] = (keeps[first] + partner.astype(F32)).astype(BF16)
    paired[0], ratio = lax.optimization_barrier((paired[0], ratio))
    parts = [moved(paired[shift], near_axes, shift) for shift in (2, 1, 3)]
    line = paired[0].astype(F32) + sum(part.astype(F32) for part in parts)
    line = line.astype(BF16)
    parts = [moved(line[shift], far_axes, shift) for shift in (2, 1, 3)]
    block = line[0].astype(F32) + sum(part.astype(F32) for part in parts)
    left, right = block[:, :rows], block[:, rows:]
    other = moved(jnp.where(on_zero, right, left), None, 0)
    mine = jnp.where(on_zero, left, right)
    gradient = jnp.stack(
        [jnp.where(on_zero, mine, other).T, jnp.where(on_zero, other, mine).T], axis=1
    )
    moment_one = BETA_ONE * first_moment[0] + (1.0 - BETA_ONE) * gradient
    moment_two = BETA_TWO * second_moment[0] + (1.0 - BETA_TWO) * gradient * gradient
    direction = moment_one / FIRST_FIX / (jnp.sqrt(moment_two / SECOND_FIX) + ADAM_EPS)
    return (moment_one[None], moment_two[None], direction[None], ratio)


def solution(mesh):
    return jax.shard_map(
        on_device,
        mesh=mesh,
        in_specs=(
            P("dp", None),
            P("dp", None),
            P("dp"),
            P("dp"),
            P("section", None),
            P("section", "dp", None, None),
            P("section", "dp", None, None),
            P("section", "dp", None, None),
        ),
        out_specs=(
            P("section", "dp", None, None),
            P("section", "dp", None, None),
            P("section", "dp", None, None),
            P("dp"),
        ),
        check_vma=False,
    )
```

```python
import jax
import jax.numpy as jnp
from jax import lax
from jax.experimental import pallas as pl
from jax.experimental.pallas import tpu as pltpu
from jax.sharding import PartitionSpec as P


SEQLEN = 64
USERS_DEV = 2
SECTIONS = 4
CHUNK = 1024
RING = 4
PIECES = RING * RING

CLIP_BOUND = 70000.0
LOSS_SCALE = 1024.0
BETA_ONE = 0.9
BETA_TWO = 0.999
FIRST_FIX = 1.0 - 0.9**50
SECOND_FIX = 1.0 - 0.999**50
ADAM_EPS = 1e-08
NORM_EPS = 1e-05

F32 = jnp.float32
BF16 = jnp.bfloat16


def dot_nn(a, b):
    return jnp.dot(a, b, preferred_element_type=F32)


def dot_nt(a, b):
    return lax.dot_general(a, b, (((1,), (1,)), ((), ())), preferred_element_type=F32)


def chain_kernel(
    scal,
    tokens,
    normed0,
    gout3,
    gram_n0,
    gram_g3,
    inv0,
    gains,
    own_col,
    own_row,
    *rest,
):
    pieces = rest[: 2 * PIECES]
    (
        ratio,
        wv,
        hs,
        rights,
        inner,
        act,
        gin,
        joint,
        sq,
        lefts,
        keep,
        give,
        wsems,
        isems,
        osems,
    ) = rest[2 * PIECES + 2 * RING :]
    keep_outs = rest[2 * PIECES : 2 * PIECES + RING]
    give_outs = rest[2 * PIECES + RING : 2 * PIECES + 2 * RING]
    nm, go = rights.at[:SECTIONS], rights.at[SECTIONS:]
    rows, width = tokens.shape
    chunks = width // CHUNK
    me, core, at_x, at_z = scal[4], scal[5], scal[6], scal[7]

    def chip_of(role, first, second):
        along_x = jnp.where(role == 0, first, second)
        along_z = jnp.where(role == 0, second, first)
        return lax.rem(at_x + along_x + RING, RING) * RING + lax.rem(at_z + along_z + RING, RING)

    def start_loads(section, which):
        slot = scal[section]
        for mine in range(2):

            @pl.when((core == which) == (mine == 1))
            def _(mine=mine):
                held = pieces[:PIECES] if mine else pieces[PIECES:]
                for index, piece in enumerate(held):
                    chip = chip_of(which, -(index % RING), -(index // RING))
                    pltpu.make_async_copy(
                        piece.at[slot],
                        wv.at[2 * section + which, pl.ds(chip * 256, 256), :],
                        wsems.at[2 * section + which],
                    ).start()

    def wait_load(section, which):
        whole = wv.at[2 * section + which]
        pltpu.make_async_copy(whole, whole, wsems.at[2 * section + which]).wait()

    start_loads(0, 0)
    first_inputs = [
        pltpu.make_async_copy(normed0, nm.at[0], isems.at[0]),
        pltpu.make_async_copy(tokens, hs.at[0], isems.at[1]),
        pltpu.make_async_copy(gout3, go.at[SECTIONS - 1], isems.at[2]),
    ]
    first_inputs[0].start()
    start_loads(0, 1)
    first_inputs[1].start()

    def later_loads(section, carry):
        start_loads(section, 0)
        start_loads(section, 1)
        return carry

    lax.fori_loop(1, SECTIONS, later_loads, 0)
    first_inputs[2].start()

    def cols(i):
        return pl.ds(pl.multiple_of(i * CHUNK, CHUNK), CHUNK)

    def each(body):
        def step(i, carry):
            body(cols(i))
            return carry

        lax.fori_loop(0, chunks, step, 0, unroll=True)

    inv = inv0[...]
    invs = [inv]
    for s in range(SECTIONS):
        wait_load(s, 0)
        slot = scal[s]
        if s == 0:
            first_inputs[0].wait()
            value = dot_nn(nm[0], wv[0])
        else:

            def norm_step(c, s=s, inv=inv, slot=slot):
                n = (hs[s, :, c].astype(F32) * inv * gains[slot, :, c]).astype(BF16)
                nm[s, :, c] = n

            each(norm_step)
            value = dot_nn(nm[s], wv[2 * s])
            joint[s] = dot_nt(nm[s], nm[s])
        inner[s] = value
        active = (value * jax.nn.sigmoid(value)).astype(BF16)
        act[s] = active
        wait_load(s, 1)
        if s < SECTIONS - 1:
            if s == 0:
                first_inputs[1].wait()
            sq[...] = jnp.zeros_like(sq)

            def up_step(c, s=s, active=active):
                old = hs[s, :, c]
                new = (old.astype(F32) + dot_nt(active, wv[2 * s + 1, c, :])).astype(BF16)
                hs[s + 1, :, c] = new
                wide = new.astype(F32)
                wide = wide * wide
                part = wide[:, :128]
                for k in range(1, CHUNK // 128):
                    part = part + wide[:, 128 * k : 128 * (k + 1)]
                sq[...] += part

            each(up_step)
            mean = jnp.sum(sq[...], axis=-1, keepdims=True) * (1.0 / width)
            inv = lax.rsqrt(mean + NORM_EPS)
            invs.append(inv)

    total = jnp.zeros((rows, rows), F32)
    for s in reversed(range(SECTIONS)):
        if s == SECTIONS - 1:
            first_inputs[2].wait()
            gact = dot_nn(go[s], wv[2 * s + 1])
            gram_g = gram_g3[...]
        else:
            gact = dot_nn(go[s], wv[2 * s + 1])
            gram_g = dot_nt(go[s], go[s])
        value = inner[s]
        sig = jax.nn.sigmoid(value)
        gi = (gact * sig * (1.0 + value * (1.0 - sig))).astype(BF16)
        gin[s] = gi
        gram_n = gram_n0[...] if s == 0 else joint[s]
        total = total + gram_n * dot_nt(gi, gi) + dot_nt(act[s], act[s]) * gram_g
        if s > 0:
            inv = invs[s]
            proj = jnp.sum(gi.astype(F32) * value, axis=-1, keepdims=True) * (1.0 / width)
            coef = inv * inv * proj
            slot = scal[s]

            def back_step(c, s=s, inv=inv, coef=coef, gi=gi, slot=slot):
                gn = dot_nt(gi, wv[2 * s, c, :])
                above = go[s, :, c]
                g = (
                    above.astype(F32)
                    + inv * (gn * gains[slot, :, c])
                    - hs[s, :, c].astype(F32) * coef
                ).astype(BF16)
                go[s - 1, :, c] = g

            each(back_step)

    factor = jnp.zeros((rows, 1), F32)
    lane = lax.broadcasted_iota(jnp.int32, (1, 128), 1)
    report = jnp.zeros((1, 128), F32)
    for u in range(USERS_DEV):
        column = own_col[:, u : u + 1]
        part = jnp.sum(total * own_row[u : u + 1, :], axis=1, keepdims=True) * column
        norm = jnp.sqrt(jnp.sum(part, axis=0, keepdims=True))
        factor = factor + column * (LOSS_SCALE / jnp.maximum(norm, CLIP_BOUND))
        report = jnp.where(lane == u, norm * (1.0 / CLIP_BOUND), report)
    ratio[...] = jnp.broadcast_to(report, ratio.shape)

    lefts[0] = jnp.transpose(gin[me].astype(F32) * factor).astype(BF16)
    lefts[1] = jnp.transpose(act[me].astype(F32) * factor).astype(BF16)

    other = 1 - core

    outs = []
    for base, which, source, targets in (
        (0, core, keep, keep_outs),
        (RING, other, give, give_outs),
    ):
        for first in range(RING):
            for second in range(RING):
                c = pl.ds(pl.multiple_of(chip_of(which, first, second) * 256, 256), 256)
                value = dot_nn(lefts[which], rights[which * SECTIONS + me, :, c])
                source[first, second] = value.astype(source.dtype)
            outs.append(
                pltpu.make_async_copy(source.at[first], targets[first], osems.at[base + first])
            )
            outs[-1].start()
    for out in outs:
        out.wait()


def run_chain(
    scal, tokens, normed0, gout3, gram_n0, gram_g3, inv0, gains, own_col, own_row, pieces
):
    rows, width = tokens.shape
    inner_width = pieces[0].shape[-1]
    vmem = pl.BlockSpec(memory_space=pltpu.VMEM)
    hbm = pl.BlockSpec(memory_space=pl.ANY)
    blocks = (RING, RING, inner_width, 256)
    return pl.pallas_call(
        chain_kernel,
        out_shape=[jax.ShapeDtypeStruct(blocks[1:], F32)] * RING
        + [jax.ShapeDtypeStruct(blocks[1:], BF16)] * RING
        + [jax.ShapeDtypeStruct((8, 128), F32)],
        in_specs=[pl.BlockSpec(memory_space=pltpu.SMEM)]
        + [hbm] * 3
        + [vmem] * 6
        + [hbm] * len(pieces),
        out_specs=[hbm] * (2 * RING) + [vmem],
        scratch_shapes=[
            pltpu.VMEM((2 * SECTIONS, width, inner_width), BF16),
            pltpu.VMEM((SECTIONS, rows, width), BF16),
            pltpu.VMEM((2 * SECTIONS, rows, width), BF16),
            pltpu.VMEM((SECTIONS, rows, inner_width), F32),
            pltpu.VMEM((SECTIONS, rows, inner_width), BF16),
            pltpu.VMEM((SECTIONS, rows, inner_width), BF16),
            pltpu.VMEM((SECTIONS, rows, rows), F32),
            pltpu.VMEM((rows, 128), F32),
            pltpu.VMEM((2, rows, inner_width), BF16),
            pltpu.VMEM(blocks, F32),
            pltpu.VMEM(blocks, BF16),
            pltpu.SemaphoreType.DMA((2 * SECTIONS,)),
            pltpu.SemaphoreType.DMA((3,)),
            pltpu.SemaphoreType.DMA((2 * RING,)),
        ],
        compiler_params=pltpu.CompilerParams(vmem_limit_bytes=54 * 1024 * 1024),
        name="chain",
    )(scal, tokens, normed0, gout3, gram_n0, gram_g3, inv0, gains, own_col, own_row, *pieces)


def moved(value, axes, shift):
    pairs = []
    for x in range(RING):
        for z in range(RING):
            for core in range(2):
                to = [x, z]
                if axes is not None:
                    to[axes[core] - 1] = (to[axes[core] - 1] + shift) % RING
                target = core if axes is not None else 1 - core
                pairs.append(((x * RING + z) * 2 + core, (to[0] * RING + to[1]) * 2 + target))
    return lax.ppermute(value, "dp", pairs)


def on_device(
    tokens, cotangent, lengths, seq_user, norm_gains, weights, first_moment, second_moment
):
    section_index = lax.axis_index("section")
    dp_index = lax.axis_index("dp")
    core = dp_index % 2
    at_x, at_z = dp_index // (2 * RING), (dp_index // 2) % RING
    tok_rows, model_width = tokens.shape
    rows = weights.shape[1]
    width = weights.shape[3]
    on_zero = core == 0
    near_axes, far_axes = (1, 2), (2, 1)

    shard = weights[0].astype(BF16)
    down, up = shard[:, 0, :], shard[:, 1, :]
    partner = moved(jnp.where(on_zero, up, down), None, 0)
    own = jnp.where(on_zero, down, up)
    gain = norm_gains[0]
    high = lax.reduce_precision(gain, 8, 7)
    middle = lax.reduce_precision(gain - high, 8, 7)
    low = gain - high - middle
    digits = jnp.stack([high, middle, low]).astype(BF16).reshape(-1, width)
    payload = jnp.concatenate(
        [jnp.where(on_zero, own, partner), jnp.where(on_zero, partner, own), digits], axis=0
    )
    held = [payload]
    for shift in (2, 1, 3):
        pairs = [(s, (s + shift) % SECTIONS) for s in range(SECTIONS)]
        held.append(lax.ppermute(payload, "section", pairs))
    held = [held[0], held[2], held[1], held[3]]
    column = jnp.stack([piece[: 2 * rows] for piece in held])
    column, cotangent = lax.optimization_barrier((column, cotangent))
    gains = jnp.stack(
        [
            jnp.sum(piece[2 * rows :].astype(F32).reshape(3, model_width), axis=0, keepdims=True)
            for piece in held
        ]
    )
    slots = (section_index - jnp.arange(SECTIONS)) % SECTIONS
    scal = jnp.concatenate([slots, jnp.stack([section_index, core, at_x, at_z])])
    scal = scal.astype(jnp.int32)

    positions = jnp.arange(tok_rows) % SEQLEN
    usable = positions < jnp.repeat(lengths, SEQLEN)
    token_user = jnp.repeat(seq_user - dp_index * USERS_DEV, SEQLEN)
    own_row = (
        (token_user[None, :] == jnp.arange(8)[:, None])
        & usable[None, :]
        & (jnp.arange(8) < USERS_DEV)[:, None]
    ).astype(F32)
    own_col = (
        (token_user[:, None] == jnp.arange(128)[None, :])
        & usable[:, None]
        & (jnp.arange(128) < USERS_DEV)[None, :]
    ).astype(F32)
    widened = tokens.astype(F32)
    inv0 = lax.rsqrt(jnp.mean(widened * widened, axis=-1, keepdims=True) + NORM_EPS)
    gain0 = lax.dynamic_index_in_dim(gains, slots[0], 0, keepdims=False)
    normed0 = (widened * inv0 * gain0).astype(BF16)
    gout3 = cotangent * usable[:, None].astype(BF16)
    gram_n0, gram_g3 = dot_nt(normed0, normed0), dot_nt(gout3, gout3)
    near = [column] + [moved(column, near_axes, shift) for shift in (1, 2, 3)]
    near[2], normed0, gout3, gram_n0, gram_g3, inv0, scal, own_row, own_col = (
        lax.optimization_barrier(
            (near[2], normed0, gout3, gram_n0, gram_g3, inv0, scal, own_row, own_col)
        )
    )
    after = [moved(near[k], far_axes, 1) for k in range(RING)]
    before = [moved(near[k], far_axes, 3) for k in range(RING)]
    across = [
        moved(after[k], far_axes, 1)
        if k < 2
        else moved(before[k], far_axes, 3)
        for k in range(RING)
    ]
    pieces = [line[k] for line in (near, after, across, before) for k in range(RING)]
    pieces = pieces + [moved(piece, None, 0) for piece in pieces]
    results = run_chain(
        scal,
        tokens,
        normed0,
        gout3,
        gram_n0,
        gram_g3,
        inv0,
        gains,
        own_col,
        own_row,
        pieces,
    )
    keeps, gives, ratio = results[:RING], results[RING : 2 * RING], results[-1][0, :USERS_DEV]
    paired = [None] * RING
    for first in (2, 1, 3, 0):
        partner = moved(gives[first], None, 0)
        paired[first] = (keeps[first] + partner.astype(F32)).astype(BF16)
    paired[0], ratio = lax.optimization_barrier((paired[0], ratio))
    parts = [moved(paired[shift], near_axes, shift) for shift in (2, 1, 3)]
    line = paired[0].astype(F32) + sum(part.astype(F32) for part in parts)
    line = line.astype(BF16)
    parts = [moved(line[shift], far_axes, shift) for shift in (2, 1, 3)]
    block = line[0].astype(F32) + sum(part.astype(F32) for part in parts)
    left, right = block[:, :rows], block[:, rows:]
    other = moved(jnp.where(on_zero, right, left), None, 0)
    mine = jnp.where(on_zero, left, right)
    gradient = jnp.stack(
        [jnp.where(on_zero, mine, other).T, jnp.where(on_zero, other, mine).T], axis=1
    )
    moment_one = BETA_ONE * first_moment[0] + (1.0 - BETA_ONE) * gradient
    moment_two = BETA_TWO * second_moment[0] + (1.0 - BETA_TWO) * gradient * gradient
    direction = moment_one / FIRST_FIX / (jnp.sqrt(moment_two / SECOND_FIX) + ADAM_EPS)
    return (moment_one[None], moment_two[None], direction[None], ratio)


def solution(mesh):
    return jax.shard_map(
        on_device,
        mesh=mesh,
        in_specs=(
            P("dp", None),
            P("dp", None),
            P("dp"),
            P("dp"),
            P("section", None),
            P("section", "dp", None, None),
            P("section", "dp", None, None),
            P("section", "dp", None, None),
        ),
        out_specs=(
            P("section", "dp", None, None),
            P("section", "dp", None, None),
            P("section", "dp", None, None),
            P("dp"),
        ),
        check_vma=False,
    )
```

```python
import jax
import jax.numpy as jnp
from jax import lax
from jax.experimental import pallas as pl
from jax.experimental.pallas import tpu as pltpu
from jax.sharding import PartitionSpec as P


SEQLEN = 64
USERS_DEV = 2
SECTIONS = 4
CHUNK = 1024
RING = 4
PIECES = RING * RING

CLIP_BOUND = 70000.0
LOSS_SCALE = 1024.0
BETA_ONE = 0.9
BETA_TWO = 0.999
FIRST_FIX = 1.0 - 0.9**50
SECOND_FIX = 1.0 - 0.999**50
ADAM_EPS = 1e-08
NORM_EPS = 1e-05

F32 = jnp.float32
BF16 = jnp.bfloat16


def dot_nn(a, b):
    return jnp.dot(a, b, preferred_element_type=F32)


def dot_nt(a, b):
    return lax.dot_general(a, b, (((1,), (1,)), ((), ())), preferred_element_type=F32)


def chain_kernel(
    scal,
    tokens,
    normed0,
    gout3,
    gram_n0,
    gram_g3,
    inv0,
    gains,
    own_col,
    own_row,
    *rest,
):
    pieces = rest[: 2 * PIECES]
    (
        ratio,
        wv,
        hs,
        rights,
        inner,
        act,
        gin,
        joint,
        sq,
        lefts,
        keep,
        give,
        wsems,
        isems,
        osems,
    ) = rest[2 * PIECES + 2 * RING :]
    keep_outs = rest[2 * PIECES : 2 * PIECES + RING]
    give_outs = rest[2 * PIECES + RING : 2 * PIECES + 2 * RING]
    nm, go = rights.at[:SECTIONS], rights.at[SECTIONS:]
    rows, width = tokens.shape
    chunks = width // CHUNK
    me, core, at_x, at_z = scal[4], scal[5], scal[6], scal[7]

    def chip_of(role, first, second):
        along_x = jnp.where(role == 0, first, second)
        along_z = jnp.where(role == 0, second, first)
        return lax.rem(at_x + along_x + RING, RING) * RING + lax.rem(at_z + along_z + RING, RING)

    def start_loads(section):
        slot = scal[section]
        for which, held in ((core, pieces[:PIECES]), (1 - core, pieces[PIECES:])):
            for index, piece in enumerate(held):
                chip = chip_of(which, -(index % RING), -(index // RING))
                pltpu.make_async_copy(
                    piece.at[slot],
                    wv.at[2 * section + which, pl.ds(chip * 256, 256), :],
                    wsems.at[2 * section + which],
                ).start()

    def wait_load(section, which):
        whole = wv.at[2 * section + which]
        pltpu.make_async_copy(whole, whole, wsems.at[2 * section + which]).wait()

    first_inputs = [
        pltpu.make_async_copy(normed0, nm.at[0], isems.at[0]),
        pltpu.make_async_copy(tokens, hs.at[0], isems.at[1]),
        pltpu.make_async_copy(gout3, go.at[SECTIONS - 1], isems.at[2]),
    ]
    first_inputs[0].start()

    def loads(section, carry):
        start_loads(section)

        @pl.when(section == 0)
        def _():
            first_inputs[1].start()

        return carry

    lax.fori_loop(0, SECTIONS, loads, 0)
    first_inputs[2].start()

    def cols(i):
        return pl.ds(pl.multiple_of(i * CHUNK, CHUNK), CHUNK)

    def each(body):
        def step(i, carry):
            body(cols(i))
            return carry

        lax.fori_loop(0, chunks, step, 0, unroll=True)

    inv = inv0[...]
    invs = [inv]
    for s in range(SECTIONS):
        wait_load(s, 0)
        slot = scal[s]
        if s == 0:
            first_inputs[0].wait()
            value = dot_nn(nm[0], wv[0])
        else:

            def norm_step(c, s=s, inv=inv, slot=slot):
                n = (hs[s, :, c].astype(F32) * inv * gains[slot, :, c]).astype(BF16)
                nm[s, :, c] = n

            each(norm_step)
            value = dot_nn(nm[s], wv[2 * s])
            joint[s] = dot_nt(nm[s], nm[s])
        inner[s] = value
        active = (value * jax.nn.sigmoid(value)).astype(BF16)
        act[s] = active
        wait_load(s, 1)
        if s < SECTIONS - 1:
            if s == 0:
                first_inputs[1].wait()
            sq[...] = jnp.zeros_like(sq)

            def up_step(c, s=s, active=active):
                old = hs[s, :, c]
                new = (old.astype(F32) + dot_nt(active, wv[2 * s + 1, c, :])).astype(BF16)
                hs[s + 1, :, c] = new
                wide = new.astype(F32)
                wide = wide * wide
                part = wide[:, :128]
                for k in range(1, CHUNK // 128):
                    part = part + wide[:, 128 * k : 128 * (k + 1)]
                sq[...] += part

            each(up_step)
            mean = jnp.sum(sq[...], axis=-1, keepdims=True) * (1.0 / width)
            inv = lax.rsqrt(mean + NORM_EPS)
            invs.append(inv)

    total = jnp.zeros((rows, rows), F32)
    for s in reversed(range(SECTIONS)):
        if s == SECTIONS - 1:
            first_inputs[2].wait()
            gact = dot_nn(go[s], wv[2 * s + 1])
            gram_g = gram_g3[...]
        else:
            gact = dot_nn(go[s], wv[2 * s + 1])
            gram_g = dot_nt(go[s], go[s])
        value = inner[s]
        sig = jax.nn.sigmoid(value)
        gi = (gact * sig * (1.0 + value * (1.0 - sig))).astype(BF16)
        gin[s] = gi
        gram_n = gram_n0[...] if s == 0 else joint[s]
        total = total + gram_n * dot_nt(gi, gi) + dot_nt(act[s], act[s]) * gram_g
        if s > 0:
            inv = invs[s]
            proj = jnp.sum(gi.astype(F32) * value, axis=-1, keepdims=True) * (1.0 / width)
            coef = inv * inv * proj
            slot = scal[s]

            def back_step(c, s=s, inv=inv, coef=coef, gi=gi, slot=slot):
                gn = dot_nt(gi, wv[2 * s, c, :])
                above = go[s, :, c]
                g = (
                    above.astype(F32)
                    + inv * (gn * gains[slot, :, c])
                    - hs[s, :, c].astype(F32) * coef
                ).astype(BF16)
                go[s - 1, :, c] = g

            each(back_step)

    factor = jnp.zeros((rows, 1), F32)
    lane = lax.broadcasted_iota(jnp.int32, (1, 128), 1)
    report = jnp.zeros((1, 128), F32)
    for u in range(USERS_DEV):
        column = own_col[:, u : u + 1]
        part = jnp.sum(total * own_row[u : u + 1, :], axis=1, keepdims=True) * column
        norm = jnp.sqrt(jnp.sum(part, axis=0, keepdims=True))
        factor = factor + column * (LOSS_SCALE / jnp.maximum(norm, CLIP_BOUND))
        report = jnp.where(lane == u, norm * (1.0 / CLIP_BOUND), report)
    ratio[...] = jnp.broadcast_to(report, ratio.shape)

    lefts[0] = jnp.transpose(gin[me].astype(F32) * factor).astype(BF16)
    lefts[1] = jnp.transpose(act[me].astype(F32) * factor).astype(BF16)

    other = 1 - core

    def emit(which, target, first):
        for second in range(RING):
            c = pl.ds(pl.multiple_of(chip_of(which, first, second) * 256, 256), 256)
            value = dot_nn(lefts[which], rights[which * SECTIONS + me, :, c])
            target[first, second] = value.astype(target.dtype)

    def emit_kept(half, carry):
        emit(core, keep, 2 * half)
        emit(core, keep, 2 * half + 1)
        return carry

    lax.fori_loop(0, RING // 2, emit_kept, 0)
    outs = [
        pltpu.make_async_copy(keep.at[first], keep_outs[first], osems.at[first])
        for first in range(RING)
    ]
    for out in outs:
        out.start()
    for first in range(RING):
        emit(other, give, first)
        outs.append(
            pltpu.make_async_copy(give.at[first], give_outs[first], osems.at[RING + first])
        )
        outs[-1].start()
    for out in outs:
        out.wait()


def run_chain(
    scal, tokens, normed0, gout3, gram_n0, gram_g3, inv0, gains, own_col, own_row, pieces
):
    rows, width = tokens.shape
    inner_width = pieces[0].shape[-1]
    vmem = pl.BlockSpec(memory_space=pltpu.VMEM)
    hbm = pl.BlockSpec(memory_space=pl.ANY)
    blocks = (RING, RING, inner_width, 256)
    return pl.pallas_call(
        chain_kernel,
        out_shape=[jax.ShapeDtypeStruct(blocks[1:], F32)] * RING
        + [jax.ShapeDtypeStruct(blocks[1:], BF16)] * RING
        + [jax.ShapeDtypeStruct((8, 128), F32)],
        in_specs=[pl.BlockSpec(memory_space=pltpu.SMEM)]
        + [hbm] * 3
        + [vmem] * 6
        + [hbm] * len(pieces),
        out_specs=[hbm] * (2 * RING) + [vmem],
        scratch_shapes=[
            pltpu.VMEM((2 * SECTIONS, width, inner_width), BF16),
            pltpu.VMEM((SECTIONS, rows, width), BF16),
            pltpu.VMEM((2 * SECTIONS, rows, width), BF16),
            pltpu.VMEM((SECTIONS, rows, inner_width), F32),
            pltpu.VMEM((SECTIONS, rows, inner_width), BF16),
            pltpu.VMEM((SECTIONS, rows, inner_width), BF16),
            pltpu.VMEM((SECTIONS, rows, rows), F32),
            pltpu.VMEM((rows, 128), F32),
            pltpu.VMEM((2, rows, inner_width), BF16),
            pltpu.VMEM(blocks, F32),
            pltpu.VMEM(blocks, BF16),
            pltpu.SemaphoreType.DMA((2 * SECTIONS,)),
            pltpu.SemaphoreType.DMA((3,)),
            pltpu.SemaphoreType.DMA((2 * RING,)),
        ],
        compiler_params=pltpu.CompilerParams(vmem_limit_bytes=54 * 1024 * 1024),
        name="chain",
    )(scal, tokens, normed0, gout3, gram_n0, gram_g3, inv0, gains, own_col, own_row, *pieces)


def moved(value, axes, shift):
    pairs = []
    for x in range(RING):
        for z in range(RING):
            for core in range(2):
                to = [x, z]
                if axes is not None:
                    to[axes[core] - 1] = (to[axes[core] - 1] + shift) % RING
                target = core if axes is not None else 1 - core
                pairs.append(((x * RING + z) * 2 + core, (to[0] * RING + to[1]) * 2 + target))
    return lax.ppermute(value, "dp", pairs)


def on_device(
    tokens, cotangent, lengths, seq_user, norm_gains, weights, first_moment, second_moment
):
    section_index = lax.axis_index("section")
    dp_index = lax.axis_index("dp")
    core = dp_index % 2
    at_x, at_z = dp_index // (2 * RING), (dp_index // 2) % RING
    tok_rows, model_width = tokens.shape
    rows = weights.shape[1]
    width = weights.shape[3]
    on_zero = core == 0
    near_axes, far_axes = (1, 2), (2, 1)

    shard = weights[0].astype(BF16)
    down, up = shard[:, 0, :], shard[:, 1, :]
    partner = moved(jnp.where(on_zero, up, down), None, 0)
    own = jnp.where(on_zero, down, up)
    gain = norm_gains[0]
    high = lax.reduce_precision(gain, 8, 7)
    middle = lax.reduce_precision(gain - high, 8, 7)
    low = gain - high - middle
    digits = jnp.stack([high, middle, low]).astype(BF16).reshape(-1, width)
    payload = jnp.concatenate(
        [jnp.where(on_zero, own, partner), jnp.where(on_zero, partner, own), digits], axis=0
    )
    held = [payload]
    for shift in (2, 1, 3):
        pairs = [(s, (s + shift) % SECTIONS) for s in range(SECTIONS)]
        held.append(lax.ppermute(payload, "section", pairs))
    held = [held[0], held[2], held[1], held[3]]
    column = jnp.stack([piece[: 2 * rows] for piece in held])
    column, cotangent = lax.optimization_barrier((column, cotangent))
    gains = jnp.stack(
        [
            jnp.sum(piece[2 * rows :].astype(F32).reshape(3, model_width), axis=0, keepdims=True)
            for piece in held
        ]
    )
    slots = (section_index - jnp.arange(SECTIONS)) % SECTIONS
    scal = jnp.concatenate([slots, jnp.stack([section_index, core, at_x, at_z])])
    scal = scal.astype(jnp.int32)

    positions = jnp.arange(tok_rows) % SEQLEN
    usable = positions < jnp.repeat(lengths, SEQLEN)
    token_user = jnp.repeat(seq_user - dp_index * USERS_DEV, SEQLEN)
    own_row = (
        (token_user[None, :] == jnp.arange(8)[:, None])
        & usable[None, :]
        & (jnp.arange(8) < USERS_DEV)[:, None]
    ).astype(F32)
    own_col = (
        (token_user[:, None] == jnp.arange(128)[None, :])
        & usable[:, None]
        & (jnp.arange(128) < USERS_DEV)[None, :]
    ).astype(F32)
    widened = tokens.astype(F32)
    inv0 = lax.rsqrt(jnp.mean(widened * widened, axis=-1, keepdims=True) + NORM_EPS)
    gain0 = lax.dynamic_index_in_dim(gains, slots[0], 0, keepdims=False)
    normed0 = (widened * inv0 * gain0).astype(BF16)
    gout3 = cotangent * usable[:, None].astype(BF16)
    gram_n0, gram_g3 = dot_nt(normed0, normed0), dot_nt(gout3, gout3)
    near = [column] + [moved(column, near_axes, shift) for shift in (1, 2, 3)]
    after = [moved(near[k], far_axes, 1) for k in range(RING)]
    before = [moved(near[k], far_axes, 3) for k in range(RING)]
    before[3], normed0, gout3, gram_n0, gram_g3, inv0, scal, own_row, own_col = (
        lax.optimization_barrier(
            (before[3], normed0, gout3, gram_n0, gram_g3, inv0, scal, own_row, own_col)
        )
    )
    across = [
        moved(after[k], far_axes, 1)
        if k < 2
        else moved(before[k], far_axes, 3)
        for k in range(RING)
    ]
    pieces = [line[k] for line in (near, after, across, before) for k in range(RING)]
    pieces = pieces + [moved(piece, None, 0) for piece in pieces]
    results = run_chain(
        scal,
        tokens,
        normed0,
        gout3,
        gram_n0,
        gram_g3,
        inv0,
        gains,
        own_col,
        own_row,
        pieces,
    )
    keeps, gives, ratio = results[:RING], results[RING : 2 * RING], results[-1][0, :USERS_DEV]
    paired = [None] * RING
    for first in (2, 1, 3, 0):
        partner = moved(gives[first], None, 0)
        paired[first] = (keeps[first] + partner.astype(F32)).astype(BF16)
    paired[0], ratio = lax.optimization_barrier((paired[0], ratio))
    parts = [moved(paired[shift], near_axes, shift) for shift in (2, 1, 3)]
    line = paired[0].astype(F32) + sum(part.astype(F32) for part in parts)
    line = line.astype(BF16)
    parts = [moved(line[shift], far_axes, shift) for shift in (2, 1, 3)]
    block = line[0].astype(F32) + sum(part.astype(F32) for part in parts)
    left, right = block[:, :rows], block[:, rows:]
    other = moved(jnp.where(on_zero, right, left), None, 0)
    mine = jnp.where(on_zero, left, right)
    gradient = jnp.stack(
        [jnp.where(on_zero, mine, other).T, jnp.where(on_zero, other, mine).T], axis=1
    )
    moment_one = BETA_ONE * first_moment[0] + (1.0 - BETA_ONE) * gradient
    moment_two = BETA_TWO * second_moment[0] + (1.0 - BETA_TWO) * gradient * gradient
    direction = moment_one / FIRST_FIX / (jnp.sqrt(moment_two / SECOND_FIX) + ADAM_EPS)
    return (moment_one[None], moment_two[None], direction[None], ratio)


def solution(mesh):
    return jax.shard_map(
        on_device,
        mesh=mesh,
        in_specs=(
            P("dp", None),
            P("dp", None),
            P("dp"),
            P("dp"),
            P("section", None),
            P("section", "dp", None, None),
            P("section", "dp", None, None),
            P("section", "dp", None, None),
        ),
        out_specs=(
            P("section", "dp", None, None),
            P("section", "dp", None, None),
            P("section", "dp", None, None),
            P("dp"),
        ),
        check_vma=False,
    )
```
